32 devices in a mesh: leaf: 4 (over y, core), sub: 8 (over z, x).
Axes of the slice: x: 2, y: 2, z: 4, core: 2. Of those that a mesh axis runs over, the one named last changes fastest.
Arguments:
- points: bfloat16 [131072, 32], P(('leaf', 'sub')), may hold values from -6 to 6
- vectors: bfloat16 [131072, 2, 128], P(('leaf', 'sub')), may hold values from -6 to 6
- inv_length: float32 [32], replicated, may hold values from 0.15 to 0.5
- order: int32 [32, 4096], P(('leaf', 'sub')), may hold values from 0 to 4095, each once within a row
- leaf_basis: bfloat16 [256, 512, 128], P(('leaf', 'sub')), may hold values from -0.25 to 0.25
- leaf_transfer: bfloat16 [256, 128, 128], P(('leaf', 'sub')), may hold values from -0.5 to 0.5
- level_transfer: bfloat16 [4, 14, 128, 128], P('leaf'), may hold values from -0.5 to 0.5
- near_list: int32 [256, 3], P(('leaf', 'sub')), may hold values from 0 to 255, as said below
- near_count: int32 [256], P(('leaf', 'sub')), may hold values from 1 to 3, as said below
- pair_list: int32 [32, 3], P(('leaf', 'sub')), may hold values from 0 to 31, as said below
- pair_count: int32 [32], P(('leaf', 'sub')), may hold values from 1 to 3, as said below
- pair_coupling: bfloat16 [32, 3, 128, 128], P(('leaf', 'sub')), may hold values from -0.3125 to 0.3125
- top_list: int32 [4, 2], P('leaf'), may hold values from 0 to 3, as said below
- top_coupling: bfloat16 [4, 2, 128, 128], P('leaf'), may hold values from -0.125 to 0.125
Outputs:
- product: float32 [131072, 2, 128], P(('leaf', 'sub'))
The draws below stay inside these ranges and needn't reach their ends.
Inputs may be any that keep to these rules, and one draw needn't show every extreme that they name: `order`: each row is a permutation. `near_list`: entry 0 of a leaf's list is the leaf itself; entries 1 and 2 are, in either order, the leaves just before and just after it in leaf order within its subtree; where one of them does not exist, the other stands in entry 1 and the leaf itself in entry 2. Only the first near_count entries of a list are used; they never repeat a leaf. Some leaf uses all 3. `pair_list`: the entries of a device node are distinct devices of its own subtree whose sub index differs from its own by 1 to 4. Only the first pair_count entries are used. Some device uses all 3. `top_list`: the entries of a subtree are distinct subtrees other than itself.
All inputs are finite; a program needn't handle non-finite values.
Results may differ from the reference program's by a relative error of at most 0.008.
Values may be sent and summed in bfloat16 or wider, within the bound.
A program may use at most 64 MiB of HBM per device.

```python
import math
import jax
import jax.numpy as jnp
from jax import lax

F = 32
R = 128
NV = 128
LEAF = 512
LPD = 8
KD = 3
REACH = 4
KS = 2
PTS_DEV = 4096
NPTS = 131072
NLEAVES = 256
N_LEAF = 4
N_SUB = 8
DEVICES = 32


def near_tables(key):
    devices = N_LEAF * N_SUB
    leaves = devices * LPD
    per_tree = N_SUB * LPD
    leaf_ids = jnp.arange(leaves, dtype=jnp.int32)
    position = leaf_ids % per_tree
    has_before = position > 0
    has_after = position < per_tree - 1
    before_id = jnp.where(has_before, leaf_ids - 1, leaf_ids)
    after_id = jnp.where(has_after, leaf_ids + 1, leaf_ids)
    flipped = jax.random.randint(jax.random.fold_in(key, 11), (leaves,), 0, 2) == 1
    first_side = jnp.where(flipped, after_id, before_id)
    second_side = jnp.where(flipped, before_id, after_id)
    first_ok = jnp.where(flipped, has_after, has_before)
    second_ok = jnp.where(flipped, has_before, has_after)
    entry_one = jnp.where(first_ok, first_side, second_side)
    both_ok = first_ok & second_ok
    entry_two = jnp.where(both_ok, second_side, leaf_ids)
    existing = 1 + (first_ok | second_ok).astype(jnp.int32) + both_ok.astype(jnp.int32)
    link_table = jnp.stack([leaf_ids, entry_one, entry_two], axis=1).astype(jnp.int32)
    device_ids = leaf_ids // LPD
    crowded = jax.random.randint(jax.random.fold_in(key, 12), (devices,), 0, 8) == 0
    chosen_tree = jax.random.randint(jax.random.fold_in(key, 13), (), 0, N_LEAF)
    chosen_sub = jax.random.randint(jax.random.fold_in(key, 14), (), 1, N_SUB - 1)
    chosen_dev = chosen_tree * N_SUB + chosen_sub
    crowded = crowded | (jnp.arange(devices, dtype=jnp.int32) == chosen_dev)
    extra = jax.random.randint(jax.random.fold_in(key, 15), (leaves,), 0, 3)
    light = jnp.minimum(existing, 1 + extra)
    used_count = jnp.where(crowded[device_ids], existing, light).astype(jnp.int32)
    return (link_table, used_count)


def draw_near_list(key, part):
    return near_tables(key)[0]


def draw_near_count(key, part):
    return near_tables(key)[1]


def pair_tables(key):
    devices = N_LEAF * N_SUB
    window_size = 2 * REACH + 1
    device_ids = jnp.arange(devices, dtype=jnp.int32)
    sub_ids = device_ids % N_SUB
    shifts = jnp.arange(window_size, dtype=jnp.int32) - REACH
    target = sub_ids[:, None] + shifts[None, :]
    usable = (target >= 0) & (target < N_SUB) & (shifts[None, :] != 0)
    random_bits = jax.random.randint(jax.random.fold_in(key, 21), (devices, window_size), 0, 1 << 20)
    scores = jnp.where(usable, random_bits * window_size + jnp.arange(window_size, dtype=jnp.int32)[None, :], -1)
    winners = lax.top_k(scores, KD)[1]
    link_table = (device_ids[:, None] + shifts[winners]).astype(jnp.int32)
    used_count = jax.random.randint(jax.random.fold_in(key, 22), (devices,), 1, KD + 1)
    chosen_dev = jax.random.randint(jax.random.fold_in(key, 23), (), 0, devices)
    used_count = jnp.where(device_ids == chosen_dev, KD, used_count).astype(jnp.int32)
    return (link_table, used_count)


def draw_pair_list(key, part):
    return pair_tables(key)[0]


def draw_pair_count(key, part):
    return pair_tables(key)[1]


def draw_top_list(key, part):
    tree_ids = jnp.arange(N_LEAF, dtype=jnp.int32)
    random_bits = jax.random.randint(jax.random.fold_in(key, 31), (N_LEAF, N_LEAF), 0, 1 << 20)
    scores = jnp.where(tree_ids[:, None] != tree_ids[None, :], random_bits * N_LEAF + tree_ids[None, :], -1)
    return lax.top_k(scores, KS)[1].astype(jnp.int32)


def block_scale(rng, dims, shards, smallest, largest):
    gain, own = 1.0, jax.random.fold_in(rng, 6)
    for dim, shards_of in shards:
        draws = jnp.exp(jax.random.uniform(jax.random.fold_in(own, dim), (shards_of,), jnp.float32, smallest / len(shards), largest / len(shards)))
        gain = gain * jnp.repeat(draws, dims[dim] // shards_of).reshape([-1 if axis == dim else 1 for axis in range(len(dims))])
    return gain


def gaussian(rng, dims, spread, most, cuts=(), held_as=jnp.bfloat16):
    drawn = jax.random.normal(rng, dims, jnp.float32) * spread
    if len(cuts) > 0:
        drawn = block_scale(rng, dims, cuts, -0.22, 0.18) * drawn
    return jnp.clip(drawn, min=-most, max=most).astype(held_as)


def setup_inputs(seed: int = 0) -> dict:
    keys = jax.random.split(jax.random.key(seed), 15)
    return {
        "points": gaussian(keys[0], (NPTS, F), 1.0, 6.0, ((0, 32),)),
        "vectors": gaussian(keys[1], (NPTS, 2, NV), 1.0, 6.0, ((0, 32),)),
        "inv_length": jnp.clip(jnp.exp(jax.random.uniform(keys[2], (F,), jnp.float32, math.log(0.15), math.log(0.5))), 0.15, 0.5),
        "order": jax.vmap(lambda own: jax.random.permutation(own, PTS_DEV))(jax.random.split(keys[3], DEVICES)).reshape((DEVICES, PTS_DEV)).astype(jnp.int32),
        "leaf_basis": gaussian(keys[4], (NLEAVES, LEAF, R), LEAF ** -0.5, 0.25, ((0, 32),)),
        "leaf_transfer": gaussian(keys[5], (NLEAVES, R, R), R ** -0.5, 0.5, ((0, 32),)),
        "level_transfer": gaussian(keys[6], (N_LEAF, 2 * N_SUB - 2, R, R), R ** -0.5, 0.5, ((0, 4),)),
        "near_list": draw_near_list(jax.random.fold_in(keys[14], 71), 0),
        "near_count": draw_near_count(jax.random.fold_in(keys[14], 71), 0),
        "pair_list": draw_pair_list(jax.random.fold_in(keys[14], 71), 0),
        "pair_count": draw_pair_count(jax.random.fold_in(keys[14], 71), 0),
        "pair_coupling": gaussian(keys[11], (DEVICES, KD, R, R), (R * KD) ** -0.5, 0.3125, ((0, 32),)),
        "top_list": draw_top_list(jax.random.fold_in(keys[14], 71), 0),
        "top_coupling": gaussian(keys[13], (N_LEAF, KS, R, R), (R * KS * N_SUB) ** -0.5, 0.125, ((0, 4),)),
    }


exact_mode = lax.Precision.HIGHEST


def kernel_tile(rows_scaled, rows_sq, cols_scaled, cols_sq):
    cross = lax.dot_general(rows_scaled, cols_scaled, (((1,), (1,)), ((), ())), preferred_element_type=jnp.float32)
    distance = rows_sq[:, None] + cols_sq[None, :] - 2.0 * cross
    return jnp.exp(-0.5 * distance).astype(jnp.bfloat16)


def reference(points, vectors, inv_length, order, leaf_basis, leaf_transfer, level_transfer, near_list, near_count, pair_list, pair_count, pair_coupling, top_list, top_coupling):
    devices = N_LEAF * N_SUB
    per_dev = LPD * LEAF
    leaves = devices * LPD
    columns = 2 * NV
    levels_count = N_SUB.bit_length() - 1
    starts = jnp.arange(devices, dtype=jnp.int32) * per_dev
    row_order = (order.astype(jnp.int32) + starts[:, None]).reshape(-1)
    ordered = vectors.reshape(devices * per_dev, columns)[row_order]
    scaled = (points[row_order].astype(jnp.float32) * inv_length[None, :]).astype(jnp.bfloat16)
    squares = jnp.sum(jnp.square(scaled.astype(jnp.float32)), axis=1)
    leaf_vals = ordered.reshape(leaves, LEAF, columns)
    scaled_leaf = scaled.reshape(leaves, LEAF, F)
    squares_leaf = squares.reshape(leaves, LEAF)
    leaf_coef = jnp.einsum("lpr,lpw->lrw", leaf_basis.astype(jnp.float32), leaf_vals.astype(jnp.float32), precision=exact_mode)
    lifted = jnp.einsum("lrs,lrw->lsw", leaf_transfer.astype(jnp.float32), leaf_coef, precision=exact_mode)
    node_coef = jnp.sum(lifted.reshape(devices, LPD, R, columns), axis=1)
    level_coef = node_coef.reshape(N_LEAF, N_SUB, R, columns)
    matrices = []
    for depth_step in range(levels_count):
        node_count = N_SUB >> depth_step
        first_node = 2 * N_SUB - 2 * node_count
        matrix = level_transfer[:, first_node:first_node + node_count].astype(jnp.float32)
        matrices.append(matrix)
        lifted_part = jnp.einsum("jnrs,jnrw->jnsw", matrix, level_coef, precision=exact_mode)
        lifted_part = lifted_part.reshape(N_LEAF, node_count // 2, 2, R, columns)
        level_coef = lifted_part[:, :, 0] + lifted_part[:, :, 1]
    top_coef = level_coef[:, 0]
    node_low = node_coef.astype(jnp.bfloat16)
    top_low = top_coef.astype(jnp.bfloat16)

    def pair_one(inputs):
        links, used_count, couplings = inputs
        running = jnp.zeros((R, columns), jnp.float32)
        for member in range(KD):
            product_term = jnp.dot(couplings[member], node_low[links[member]], preferred_element_type=jnp.float32)
            running = running + jnp.where(member < used_count, product_term, 0.0)
        return running

    pair_field = lax.map(pair_one, (pair_list, pair_count, pair_coupling))
    picked = top_low[top_list]
    top_field = jnp.einsum("skrt,sktw->srw", top_coupling.astype(jnp.float32), picked.astype(jnp.float32), precision=exact_mode)
    down_field = top_field[:, None]
    for depth_step in reversed(range(levels_count)):
        down_field = jnp.repeat(down_field, 2, axis=1)
        down_field = jnp.einsum("jnrs,jnsw->jnrw", matrices[depth_step], down_field, precision=exact_mode)
    node_field = down_field.reshape(devices, R, columns) + pair_field
    leaf_field = jnp.einsum("dlrs,dsw->dlrw", leaf_transfer.astype(jnp.float32).reshape(devices, LPD, R, R), node_field, precision=exact_mode)
    leaf_field = leaf_field.reshape(leaves, R, columns).astype(jnp.bfloat16)
    far_sum = jnp.einsum("lpr,lrw->lpw", leaf_basis.astype(jnp.float32), leaf_field.astype(jnp.float32), precision=exact_mode)

    def near_one(inputs):
        leaf_index, near_links, near_used = inputs
        rows_scaled = scaled_leaf[leaf_index]
        rows_sq = squares_leaf[leaf_index]

        def add_member(member, running):
            target = near_links[member]
            tile = kernel_tile(rows_scaled, rows_sq, scaled_leaf[target], squares_leaf[target])
            return running + jnp.dot(tile, leaf_vals[target], preferred_element_type=jnp.float32)

        return lax.fori_loop(jnp.int32(0), near_used, add_member, jnp.zeros((LEAF, columns), jnp.float32))

    near_sum = lax.map(near_one, (jnp.arange(leaves, dtype=jnp.int32), near_list, near_count))
    leaf_sum = far_sum + near_sum
    result = jnp.zeros((devices * per_dev, columns), jnp.float32).at[row_order].set(leaf_sum.reshape(-1, columns))
    return result.reshape(devices * per_dev, 2, NV)
```

```python
import functools
import math

import jax
import jax.numpy as jnp
from jax import lax
from jax.experimental import pallas as pl
from jax.experimental.pallas import tpu as pltpu
from jax.sharding import PartitionSpec as P

MESH = pl.DeviceIdType.MESH
LOG2E = math.log2(math.e)
F32 = jnp.float32
BF16 = jnp.bfloat16
LANES = 128
SLICES = 8
DEPTH = 16
STEP = 512


def dot(a, b, dims):
    return lax.dot_general(a, b, ((dims[:1], dims[1:]), ((), ())), preferred_element_type=F32)


def bf16_parts(value):
    high = value.astype(BF16).astype(F32)
    rest = value - high
    mid = rest.astype(BF16).astype(F32)
    low = (rest - mid).astype(BF16).astype(F32)
    return high, mid, low


def tile_of(lhs, rhs, turned):
    return jnp.exp2(dot(lhs, rhs, (1, 0 if turned else 1))).astype(BF16)


def sides(x):
    features, count = x.shape
    half = bf16_parts((-0.5 * LOG2E) * jnp.sum(x * x, axis=0, keepdims=True))
    ones = jnp.ones((3, count), F32)
    pad = jnp.zeros((2, count), F32)
    rest = jnp.zeros((LANES - 3 * features - 8, count), F32)
    left = jnp.concatenate([*bf16_parts(x * LOG2E), jnp.concatenate([*half, ones, pad], axis=0), rest], axis=0)
    right = jnp.concatenate([x, x, x, jnp.concatenate([ones, *half, pad], axis=0), rest], axis=0)
    return left.astype(BF16), right.astype(BF16)


def take_rows(order_ref, table, start, out):
    step = SLICES * DEPTH

    @pl.loop(0, out.shape[0] // step)
    def _(i):
        bases = [i * step + q * DEPTH for q in range(SLICES)]
        places = [order_ref.at[pl.ds(start + base, DEPTH)] for base in bases]
        targets = [out.at[pl.ds(base, DEPTH)] for base in bases]
        for k in range(DEPTH):
            for place, target in zip(places, targets):
                target[k] = table[place[k]]


def near_kernel(
    subs, tops,
    order_hbm, twice_src, list_hbm, count_hbm, pairs_hbm, used_hbm, tops_hbm,
    vec_hbm, pts_hbm, inv_hbm, basis_hbm, transfer_hbm, level_hbm, pair_hbm, top_hbm,
    near_hbm, field_ref, twice_hbm,
    order_ref, near_list, near_count, pair_list, pair_count, top_list,
    vec_ref, pts_ref, inv_ref, basis_ref, transfer_ref, level_ref, pair_ref, top_ref,
    load_sem, near_ref, near_sem,
    order_vec, twice_sem, table, got, ordered, feat, edge_feat, node_sum, node_low,
    halo_feat, halo_vals, nodes, top_low, top_all, part_low, mate_low,
    node_send, node_recv, pass_send, pass_recv, halo_send, halo_recv, top_send, top_recv,
):
    leaves, rows, rank = basis_ref.shape
    features, count = pts_ref.shape
    columns = ordered.shape[2]
    sub = lax.axis_index("sub")
    top = lax.axis_index("leaf")
    levels = subs.bit_length() - 1
    first_leaf = (top * subs + sub) * leaves
    mate = sub + 1 - 2 * lax.rem(sub, 2)

    loads = [
        pltpu.make_async_copy(src, dst, load_sem.at[n])
        for n, (src, dst) in enumerate((
            (vec_hbm, vec_ref), (order_hbm, order_ref), (basis_hbm, basis_ref),
            (transfer_hbm, transfer_ref), (pts_hbm, pts_ref), (inv_hbm, inv_ref),
            (twice_src, order_vec), (level_hbm, level_ref),
            (pair_hbm, pair_ref), (top_hbm, top_ref), (list_hbm, near_list),
            (count_hbm, near_count), (pairs_hbm, pair_list), (used_hbm, pair_count),
            (tops_hbm, top_list),
        ))
    ]
    for load in loads:
        load.start()

    barrier = pltpu.get_barrier_semaphore()
    for d in range(1, subs):
        pl.semaphore_signal(barrier, inc=1, device_id={"sub": lax.rem(sub + d, subs)}, device_id_type=MESH)
    for d in range(1, tops):
        pl.semaphore_signal(barrier, inc=1, device_id={"leaf": lax.rem(top + d, tops)}, device_id_type=MESH)

    def fetch(leaf):
        take_rows(order_ref, vec_ref, leaf * rows, got)
        ordered[leaf] = got[...].reshape(rows, columns)

    def lift(leaf):
        coef = dot(basis_ref[leaf], ordered[leaf], (0, 0)).astype(BF16)
        node_sum[...] = node_sum[...] + dot(transfer_ref[leaf], coef, (0, 0))

    node_sum[...] = jnp.zeros_like(node_sum)
    for load in loads[:2]:
        load.wait()
    fetch(leaves - 1)
    fetch(0)
    pl.semaphore_wait(barrier, subs + tops - 2)

    def halo_copy(side, n):
        leaf, peer = (leaves - 1, sub + 1) if side == 0 else (0, sub - 1)
        src, dst = ((ordered.at[leaf], halo_vals.at[side]), (edge_feat.at[side], halo_feat.at[side]))[n]
        return pltpu.make_async_remote_copy(
            src_ref=src, dst_ref=dst,
            send_sem=halo_send.at[2 * side + n], recv_sem=halo_recv.at[2 * side + n],
            device_id={"sub": jnp.clip(peer, 0, subs - 1)}, device_id_type=MESH,
        )

    sends = (sub < subs - 1, sub > 0)
    for side in range(2):
        @pl.when(sends[side])
        def _():
            halo_copy(side, 0).start()

        @pl.when(jnp.logical_not(sends[1 - side]))
        def _():
            halo_feat[side] = jnp.zeros(halo_feat.shape[1:], BF16)
            halo_vals[side] = jnp.zeros(halo_vals.shape[1:], BF16)

    for load in loads[2:4]:
        load.wait()
    lift(leaves - 1)
    lift(0)

    @pl.loop(1, leaves - 1)
    def _(leaf):
        fetch(leaf)
        lift(leaf)

    node = node_sum[...].astype(BF16)
    node_low[...] = node
    nodes[sub] = node

    def node_copy(n, src, dst, peer, sends_to, recvs):
        return pltpu.make_async_remote_copy(
            src_ref=src, dst_ref=dst, send_sem=sends_to.at[n], recv_sem=recvs.at[n],
            device_id={"sub": peer}, device_id_type=MESH,
        )

    half = subs // 2
    to_mate = [node_copy(0, node_low, nodes.at[sub], mate, pass_send, pass_recv)]
    to_mate[0].start()
    along = []
    for d in range(1, half):
        copy = node_copy(d - 1, node_low, nodes.at[sub], lax.rem(sub + 2 * d, subs), node_send, node_recv)
        copy.start()
        along.append(copy)

    for load in loads[4:]:
        load.wait()
    order_vec[...] = order_vec[...] * 2
    twice_copy = pltpu.make_async_copy(order_vec, twice_hbm, twice_sem)
    twice_copy.start()

    square = (features, features)
    same = lax.broadcasted_iota(jnp.int32, square, 0) == lax.broadcasted_iota(jnp.int32, square, 1)
    inv = jnp.sum(jnp.where(same, jnp.broadcast_to(inv_ref[...], square), 0.0), axis=1, keepdims=True)

    @pl.loop(0, count // STEP)
    def _(i):
        for part in range(STEP // LANES):
            start = pl.multiple_of(i * STEP + part * LANES, LANES)
            x = (pts_ref[:, pl.ds(start, LANES)].astype(F32) * inv).astype(BF16).astype(F32)
            both = jnp.concatenate(sides(x), axis=0).T
            table[pl.ds(start, LANES)] = both.reshape(LANES, 2, LANES)

    def features_of(leaf):
        take_rows(order_ref, table, leaf * rows, got)
        feat[leaf] = got[...].reshape(rows, 2 * LANES)

    for side, leaf in ((0, leaves - 1), (1, 0)):
        features_of(leaf)
        edge_feat[side] = feat[leaf][:, LANES:].T[:features]

        @pl.when(sends[side])
        def _():
            halo_copy(side, 1).start()

    @pl.loop(1, leaves - 1)
    def _(leaf):
        features_of(leaf)

    def wanted(leaf, target):
        found = jnp.int32(0)
        for k in range(near_list.shape[0]):
            found = found | ((near_list[k, leaf] == target) & (k < near_count[leaf])).astype(jnp.int32)
        return found.astype(F32).astype(BF16)

    def near_copy(leaf):
        return pltpu.make_async_copy(near_ref.at[leaf], near_hbm.at[leaf], near_sem.at[leaf])

    def near(leaf, before, after):
        flag_before = wanted(leaf, first_leaf + leaf - 1)
        flag_after = wanted(leaf, first_leaf + leaf + 1)
        tiles, values = [], []
        for (rhs, turned, vals), flag in (
            ((feat[leaf][:, LANES:], False, ordered[leaf]), None),
            (before, flag_before),
            (after, flag_after),
        ):
            tiles.append(tile_of(feat[leaf][:, :LANES], rhs, turned))
            values.append(vals if flag is None else vals * flag)
        near_ref[leaf] = dot(jnp.concatenate(tiles, axis=1), jnp.concatenate(values, axis=0), (1, 0))
        near_copy(leaf).start()

    def own(leaf):
        return feat[leaf][:, LANES:], False, ordered[leaf]

    def inner(leaf):
        near(leaf, own(leaf - 1), own(leaf + 1))

    early, middle = leaves // 2, leaves - 2

    @pl.loop(1, early)
    def _(leaf):
        inner(leaf)

    for copy in along:
        copy.wait_recv()
    parity = lax.rem(sub, 2)
    coefs = [dot(level_ref[2 * j + parity], nodes[2 * j + parity], (0, 0)) for j in range(half)]
    for level in range(1, levels):
        width = subs >> level
        first = 2 * subs - 2 * width
        parents = []
        for j in range(width // 2):
            matrix = level_ref[first + 2 * j:first + 2 * j + 2].reshape(2 * rank, rank)
            both = jnp.concatenate([coefs[2 * j], coefs[2 * j + 1]], axis=0).astype(BF16)
            parents.append(dot(matrix, both, (0, 0)))
        coefs = parents
    part = coefs[0].astype(BF16)
    part_low[...] = part
    part_copy = node_copy(half, part_low, mate_low, mate, pass_send, pass_recv)
    part_copy.start()

    @pl.loop(early, middle)
    def _(leaf):
        inner(leaf)

    part_copy.wait_recv()
    root = (part_low[...].astype(F32) + mate_low[...].astype(F32)).astype(BF16)
    top_low[...] = root
    top_all[top] = root
    top_copies = []
    for d in range(1, tops):
        copy = pltpu.make_async_remote_copy(
            src_ref=top_low, dst_ref=top_all.at[top],
            send_sem=top_send.at[d - 1], recv_sem=top_recv.at[d - 1],
            device_id={"leaf": lax.rem(top + d, tops)}, device_id_type=MESH,
        )
        copy.start()
        top_copies.append(copy)
    for d in range(1, half):
        origin = lax.rem(sub - 2 * d + subs, subs)
        copy = node_copy(d, nodes.at[origin], nodes.at[origin], mate, pass_send, pass_recv)
        copy.start()
        to_mate.append(copy)

    @pl.loop(middle, leaves - 1)
    def _(leaf):
        inner(leaf)

    for side in range(2):
        @pl.when(sends[1 - side])
        def _():
            for n in range(2):
                halo_copy(side, n).wait_recv()

    def halo(side):
        return sides(halo_feat[side].astype(F32))[1], True, halo_vals[side]

    near(0, halo(0), own(1))
    near(leaves - 1, own(leaves - 2), halo(1))

    for copy in to_mate:
        copy.wait_recv()
    pair_field = jnp.zeros((rank, columns), F32)
    for k in range(pair_list.shape[1]):
        source = nodes[jnp.clip(pair_list[0, k] - top * subs, 0, subs - 1)]
        term = dot(pair_ref[k], source, (1, 0))
        pair_field = pair_field + jnp.where(k < pair_count[0], term, 0.0)

    for copy in top_copies:
        copy.wait_recv()
    field = jnp.zeros((rank, columns), F32)
    for k in range(top_list.shape[1]):
        field = field + dot(top_ref[k], top_all[jnp.clip(top_list[0, k], 0, tops - 1)], (1, 0))
    for level in reversed(range(levels)):
        place = 2 * subs - 2 * (subs >> level) + jnp.right_shift(sub, level)
        field = dot(level_ref[place], field.astype(BF16), (1, 0))
    field = (field + pair_field).astype(BF16)
    for leaf in range(leaves):
        field_ref[leaf] = dot(transfer_ref[leaf], field, (1, 0)).astype(BF16)

    twice_copy.wait()
    for leaf in range(leaves):
        near_copy(leaf).wait()
    for copy in along + to_mate + top_copies + [part_copy]:
        copy.wait_send()
    for side in range(2):
        @pl.when(sends[side])
        def _():
            for n in range(2):
                halo_copy(side, n).wait_send()


def scatter_kernel(twice_ref, near_ref, basis_ref, field_ref, out_ref, mixed):
    _, rows, rank = basis_ref.shape
    lanes = out_ref.shape[1]
    first = pl.program_id(0) * rows
    total = near_ref[0] + dot(basis_ref[0], field_ref[0], (1, 0))
    mixed[pl.ds(0, rows, stride=2), :] = total[:, :lanes]
    mixed[pl.ds(1, rows, stride=2), :] = total[:, lanes:]
    step = SLICES * DEPTH

    @pl.loop(0, rows // step)
    def _(i):
        bases = [i * step + q * DEPTH for q in range(SLICES)]
        places = [twice_ref.at[pl.ds(first + base, DEPTH)] for base in bases]
        sources = [mixed.at[pl.ds(base * 2, DEPTH * 2)] for base in bases]
        for k in range(DEPTH):
            taken = [source[pl.ds(2 * k, 2), :] for source in sources]
            for place, rows_of in zip(places, taken):
                out_ref[pl.ds(place[k], 2), :] = rows_of


def per_device(
    subs, tops,
    points, vectors, inv_length, order, leaf_basis, leaf_transfer, level_transfer,
    near_list, near_count, pair_list, pair_count, pair_coupling, top_list, top_coupling,
):
    leaves, rows, rank = leaf_basis.shape
    count, features = points.shape
    lanes = vectors.shape[2]
    columns = vectors.shape[1] * lanes
    smem = pl.BlockSpec(memory_space=pltpu.SMEM)
    vmem = pl.BlockSpec(memory_space=pltpu.VMEM)
    order_flat = order.reshape(-1)

    operands = (
        order_flat, order_flat.reshape(-1, LANES), near_list.T, near_count, pair_list, pair_count, top_list,
        vectors, points.T, inv_length[None, :],
        leaf_basis, leaf_transfer, level_transfer[0], pair_coupling[0], top_coupling[0],
    )
    near_sum, leaf_field, twice = pl.pallas_call(
        functools.partial(near_kernel, subs, tops),
        name="near",
        out_shape=(
            jax.ShapeDtypeStruct((leaves, rows, columns), F32),
            jax.ShapeDtypeStruct((leaves, rank, columns), BF16),
            jax.ShapeDtypeStruct((count // LANES, LANES), jnp.int32),
        ),
        in_specs=[pl.BlockSpec(memory_space=pltpu.HBM)] * len(operands),
        out_specs=(pl.BlockSpec(memory_space=pltpu.HBM), vmem, pl.BlockSpec(memory_space=pltpu.HBM)),
        scratch_shapes=[
            *(pltpu.SMEM(v.shape, v.dtype) for v in (operands[0], *operands[2:7])),
            *(pltpu.VMEM(v.shape, v.dtype) for v in operands[7:]),
            pltpu.SemaphoreType.DMA((len(operands),)),
            pltpu.VMEM((leaves, rows, columns), F32),
            pltpu.SemaphoreType.DMA((leaves,)),
            pltpu.VMEM((count // LANES, LANES), jnp.int32),
            pltpu.SemaphoreType.DMA,
            pltpu.VMEM((count, 2, LANES), BF16),
            pltpu.VMEM((rows, 2, LANES), BF16),
            pltpu.VMEM((leaves, rows, columns), BF16),
            pltpu.VMEM((leaves, rows, 2 * LANES), BF16),
            pltpu.VMEM((2, features, rows), BF16),
            pltpu.VMEM((rank, columns), F32),
            pltpu.VMEM((rank, columns), BF16),
            pltpu.VMEM((2, features, rows), BF16),
            pltpu.VMEM((2, rows, columns), BF16),
            pltpu.VMEM((subs, rank, columns), BF16),
            pltpu.VMEM((rank, columns), BF16),
            pltpu.VMEM((tops, rank, columns), BF16),
            pltpu.VMEM((rank, columns), BF16),
            pltpu.VMEM((rank, columns), BF16),
            pltpu.SemaphoreType.DMA((subs // 2 - 1,)),
            pltpu.SemaphoreType.DMA((subs // 2 - 1,)),
            pltpu.SemaphoreType.DMA((subs // 2 + 1,)),
            pltpu.SemaphoreType.DMA((subs // 2 + 1,)),
            pltpu.SemaphoreType.DMA((4,)),
            pltpu.SemaphoreType.DMA((4,)),
            pltpu.SemaphoreType.DMA((tops - 1,)),
            pltpu.SemaphoreType.DMA((tops - 1,)),
        ],
        compiler_params=pltpu.CompilerParams(
            collective_id=0, has_side_effects=True
        ),
    )(*operands)

    result = pl.pallas_call(
        scatter_kernel,
        name="scatter",
        out_shape=jax.ShapeDtypeStruct((count * 2, lanes), F32),
        grid=(leaves,),
        in_specs=[
            smem,
            pl.BlockSpec((1, rows, columns), lambda i: (i, 0, 0)),
            pl.BlockSpec((1, rows, rank), lambda i: (i, 0, 0)),
            pl.BlockSpec((1, rank, columns), lambda i: (i, 0, 0)),
        ],
        out_specs=pl.BlockSpec((count * 2, lanes), lambda i: (0, 0)),
        scratch_shapes=[pltpu.VMEM((rows * 2, lanes), F32)],
    )(twice.reshape(-1), near_sum, leaf_basis, leaf_field)
    return result.reshape(count, vectors.shape[1], lanes)


def solution(mesh):
    shape = dict(mesh.shape)
    both = ("leaf", "sub")
    return jax.shard_map(
        functools.partial(per_device, shape["sub"], shape["leaf"]),
        mesh=mesh,
        in_specs=(
            P(both, None), P(both, None, None), P(), P(both, None), P(both, None, None),
            P(both, None, None), P("leaf", None, None, None), P(both, None), P(both),
            P(both, None), P(both), P(both, None, None, None), P("leaf", None),
            P("leaf", None, None, None),
        ),
        out_specs=P(both, None, None),
        check_vma=False,
    )
```

```python
import functools
import math

import jax
import jax.numpy as jnp
from jax import lax
from jax.experimental import pallas as pl
from jax.experimental.pallas import tpu as pltpu
from jax.sharding import PartitionSpec as P

MESH = pl.DeviceIdType.MESH
LOG2E = math.log2(math.e)
F32 = jnp.float32
BF16 = jnp.bfloat16
LANES = 128
SLICES = 8
DEPTH = 16
STEP = 512


def dot(a, b, dims):
    return lax.dot_general(a, b, ((dims[:1], dims[1:]), ((), ())), preferred_element_type=F32)


def bf16_parts(value):
    high = value.astype(BF16).astype(F32)
    rest = value - high
    mid = rest.astype(BF16).astype(F32)
    low = (rest - mid).astype(BF16).astype(F32)
    return high, mid, low


def tile_of(lhs, rhs, turned):
    return jnp.exp2(dot(lhs, rhs, (1, 0 if turned else 1))).astype(BF16)


def sides(x):
    features, count = x.shape
    half = bf16_parts((-0.5 * LOG2E) * jnp.sum(x * x, axis=0, keepdims=True))
    ones = jnp.ones((3, count), F32)
    pad = jnp.zeros((2, count), F32)
    rest = jnp.zeros((LANES - 3 * features - 8, count), F32)
    left = jnp.concatenate([*bf16_parts(x * LOG2E), jnp.concatenate([*half, ones, pad], axis=0), rest], axis=0)
    right = jnp.concatenate([x, x, x, jnp.concatenate([ones, *half, pad], axis=0), rest], axis=0)
    return left.astype(BF16), right.astype(BF16)


def take_rows(order_ref, table, start, out):
    step = SLICES * DEPTH

    @pl.loop(0, out.shape[0] // step)
    def _(i):
        bases = [i * step + q * DEPTH for q in range(SLICES)]
        places = [order_ref.at[pl.ds(start + base, DEPTH)] for base in bases]
        targets = [out.at[pl.ds(base, DEPTH)] for base in bases]
        for k in range(DEPTH):
            for place, target in zip(places, targets):
                target[k] = table[place[k]]


def split_rows(got, out, leaf):
    flat = got.reshape(2 * got.shape[0], LANES)
    for half in range(2):
        out[leaf, :, half * LANES:(half + 1) * LANES] = flat[pl.ds(half, got.shape[0], stride=2), :]


def near_kernel(
    subs, tops,
    order_hbm, twice_src, list_hbm, count_hbm, pairs_hbm, used_hbm, tops_hbm,
    vec_hbm, pts_hbm, inv_hbm, basis_hbm, transfer_hbm, level_hbm, pair_hbm, top_hbm,
    near_hbm, field_hbm, twice_hbm,
    order_ref, near_list, near_count, pair_list, pair_count, top_list,
    vec_ref, pts_ref, inv_ref, basis_ref, transfer_ref, level_ref, pair_ref, top_ref,
    load_sem, near_ref, near_sem,
    field_ref, order_vec, twice_sem, table, got, ordered, feat, edge_feat, node_sum, node_low,
    halo_feat, halo_vals, nodes, part_out, part_in, top_low, top_all, down_out, down_in,
    part_send, part_recv, down_send, down_recv, fore_send, fore_recv, field_sem,
    node_send, node_recv, pass_send, pass_recv, halo_send, halo_recv, top_send, top_recv,
):
    leaves, rows, rank = basis_ref.shape
    features, count = pts_ref.shape
    columns = ordered.shape[2]
    sub = lax.axis_index("sub")
    top = lax.axis_index("leaf")
    levels = subs.bit_length() - 1
    first_leaf = (top * subs + sub) * leaves
    mate = sub + 1 - 2 * lax.rem(sub, 2)

    loads = [
        pltpu.make_async_copy(src, dst, load_sem.at[n])
        for n, (src, dst) in enumerate((
            (vec_hbm, vec_ref), (order_hbm, order_ref), (basis_hbm, basis_ref),
            (transfer_hbm, transfer_ref), (pts_hbm, pts_ref), (inv_hbm, inv_ref),
            (twice_src, order_vec), (level_hbm, level_ref),
            (pair_hbm, pair_ref), (top_hbm, top_ref), (list_hbm, near_list),
            (count_hbm, near_count), (pairs_hbm, pair_list), (used_hbm, pair_count),
            (tops_hbm, top_list),
        ))
    ]
    for load in loads:
        load.start()

    barrier = pltpu.get_barrier_semaphore()
    for d in range(1, subs):
        pl.semaphore_signal(barrier, inc=1, device_id={"sub": lax.rem(sub + d, subs)}, device_id_type=MESH)
    for d in range(1, tops):
        pl.semaphore_signal(barrier, inc=1, device_id={"leaf": lax.rem(top + d, tops)}, device_id_type=MESH)

    def fetch(leaf):
        take_rows(order_ref, vec_ref, leaf * rows, got)
        split_rows(got, ordered, leaf)

    def lift(leaf):
        coef = dot(basis_ref[leaf], ordered[leaf], (0, 0)).astype(BF16)
        node_sum[...] = node_sum[...] + dot(transfer_ref[leaf], coef, (0, 0))

    node_sum[...] = jnp.zeros_like(node_sum)
    for load in loads[:2]:
        load.wait()
    fetch(leaves - 1)
    fetch(0)
    for load in loads[2:4]:
        load.wait()
    lift(leaves - 1)
    lift(0)

    @pl.loop(1, leaves // 2 - 1)
    def _(leaf):
        fetch(leaf)
        lift(leaf)

    pl.semaphore_wait(barrier, subs + tops - 2)

    def halo_copy(side, n):
        leaf, peer = (leaves - 1, sub + 1) if side == 0 else (0, sub - 1)
        part = pl.ds(n % 2 * (rows // 2), rows // 2)
        src, dst = (
            (ordered.at[leaf, part], halo_vals.at[side, part]),
            (ordered.at[leaf, part], halo_vals.at[side, part]),
            (edge_feat.at[side], halo_feat.at[side]),
        )[n]
        return pltpu.make_async_remote_copy(
            src_ref=src, dst_ref=dst,
            send_sem=halo_send.at[3 * side + n], recv_sem=halo_recv.at[3 * side + n],
            device_id={"sub": jnp.clip(peer, 0, subs - 1)}, device_id_type=MESH,
        )

    sends = (sub < subs - 1, sub > 0)
    for side in range(2):
        @pl.when(sends[side])
        def _():
            halo_copy(side, 0).start()

        @pl.when(jnp.logical_not(sends[1 - side]))
        def _():
            halo_feat[side] = jnp.zeros(halo_feat.shape[1:], BF16)
            halo_vals[side] = jnp.zeros(halo_vals.shape[1:], BF16)

    @pl.loop(leaves // 2 - 1, leaves - 1)
    def _(leaf):
        fetch(leaf)
        lift(leaf)

    node = node_sum[...].astype(BF16)
    node_low[...] = node
    nodes[sub] = node

    for load in loads[4:]:
        load.wait()

    width = columns // subs
    kind = part_out.dtype
    raised = dot(node, level_ref[sub], (0, 0))
    for level in range(1, levels):
        place = 2 * subs - 2 * (subs >> level) + jnp.right_shift(sub, level)
        raised = dot(raised.astype(BF16), level_ref[place], (1, 0))
    for j in range(subs):
        part_out[j] = raised[j * width:(j + 1) * width].astype(kind)

    def deal(source, target, sends_to, recvs):
        copies = []
        for d in range(1, subs):
            peer = lax.rem(sub + d, subs)
            copies.append(pltpu.make_async_remote_copy(
                src_ref=source.at[peer], dst_ref=target.at[sub],
                send_sem=sends_to.at[d - 1], recv_sem=recvs.at[d - 1],
                device_id={"sub": peer}, device_id_type=MESH,
            ))
        for copy in copies:
            copy.start()
        target[sub] = source[sub]
        return copies

    part_copies = deal(part_out, part_in, part_send, part_recv)

    def node_copy(n, src, dst, peer, sends_to, recvs):
        return pltpu.make_async_remote_copy(
            src_ref=src, dst_ref=dst, send_sem=sends_to.at[n], recv_sem=recvs.at[n],
            device_id={"sub": peer}, device_id_type=MESH,
        )

    half = subs // 2
    to_mate = [node_copy(0, node_low, nodes.at[sub], mate, pass_send, pass_recv)]
    to_mate[0].start()
    along = []
    for d in reversed(range(1, half)):
        copy = node_copy(d - 1, node_low, nodes.at[sub], lax.rem(sub + 2 * d, subs), node_send, node_recv)
        copy.start()
        along.append(copy)
    for side in range(2):
        @pl.when(sends[side])
        def _():
            halo_copy(side, 1).start()

    order_vec[...] = order_vec[...] * 2
    twice_copy = pltpu.make_async_copy(order_vec, twice_hbm, twice_sem)
    twice_copy.start()

    square = (features, features)
    same = lax.broadcasted_iota(jnp.int32, square, 0) == lax.broadcasted_iota(jnp.int32, square, 1)
    inv = jnp.sum(jnp.where(same, jnp.broadcast_to(inv_ref[...], square), 0.0), axis=1, keepdims=True)

    @pl.loop(0, count // STEP)
    def _(i):
        for part in range(STEP // LANES):
            start = pl.multiple_of(i * STEP + part * LANES, LANES)
            x = (pts_ref[:, pl.ds(start, LANES)].astype(F32) * inv).astype(BF16).astype(F32)
            both = jnp.concatenate(sides(x), axis=0).T
            table[pl.ds(start, LANES)] = both.reshape(LANES, 2, LANES)

    def features_of(leaf):
        take_rows(order_ref, table, leaf * rows, got)
        split_rows(got, feat, leaf)

    for side, leaf in ((0, leaves - 1), (1, 0)):
        features_of(leaf)
        edge_feat[side] = feat[leaf][:, LANES:].T[:features]

        @pl.when(sends[side])
        def _():
            halo_copy(side, 2).start()

    @pl.loop(1, leaves - 1)
    def _(leaf):
        features_of(leaf)

    def wanted(leaf, target):
        found = jnp.int32(0)
        for k in range(near_list.shape[0]):
            found = found | ((near_list[k, leaf] == target) & (k < near_count[leaf])).astype(jnp.int32)
        return found.astype(F32).astype(BF16)

    def near_copy(leaf):
        return pltpu.make_async_copy(near_ref.at[leaf], near_hbm.at[leaf], near_sem.at[leaf])

    def near(leaf, before, after):
        flag_before = wanted(leaf, first_leaf + leaf - 1)
        flag_after = wanted(leaf, first_leaf + leaf + 1)
        tiles, values = [], []
        for (rhs, turned, vals), flag in (
            ((feat[leaf][:, LANES:], False, ordered[leaf]), None),
            (before, flag_before),
            (after, flag_after),
        ):
            tiles.append(tile_of(feat[leaf][:, :LANES], rhs, turned))
            values.append(vals if flag is None else vals * flag)
        near_ref[leaf] = dot(jnp.concatenate(tiles, axis=1), jnp.concatenate(values, axis=0), (1, 0))
        near_copy(leaf).start()

    def own(leaf):
        return feat[leaf][:, LANES:], False, ordered[leaf]

    def inner(leaf):
        near(leaf, own(leaf - 1), own(leaf + 1))

    along[0].wait_recv()
    for d in range(half - 1, half):
        origin = lax.rem(sub - 2 * d + subs, subs)
        copy = node_copy(1, nodes.at[origin], nodes.at[origin], mate, pass_send, pass_recv)
        copy.start()
        to_mate.append(copy)

    third = (leaves - 2) // 3

    @pl.loop(1, 1 + third)
    def _(leaf):
        inner(leaf)

    for copy in part_copies:
        copy.wait_recv()
    root = part_in[0].astype(F32)
    for j in range(1, subs):
        root = root + part_in[j].astype(F32)
    root = root.astype(BF16).astype(kind)
    top_low[...] = root
    top_all[top] = root
    top_copies = []
    for d in range(1, tops):
        copy = pltpu.make_async_remote_copy(
            src_ref=top_low, dst_ref=top_all.at[top],
            send_sem=top_send.at[d - 1], recv_sem=top_recv.at[d - 1],
            device_id={"leaf": lax.rem(top + d, tops)}, device_id_type=MESH,
        )
        copy.start()
        top_copies.append(copy)

    to_mate[0].wait_recv()
    passed = []
    for d in range(1, half - 1):
        copy = node_copy(d - 1, nodes.at[mate], nodes.at[mate], lax.rem(sub + 2 * d, subs), fore_send, fore_recv)
        copy.start()
        passed.append(copy)

    @pl.loop(1 + third, 1 + 2 * third)
    def _(leaf):
        inner(leaf)

    for copy in top_copies:
        copy.wait_recv()
    field = jnp.zeros((width, rank), F32)
    for k in range(top_list.shape[1]):
        found = top_all[jnp.clip(top_list[0, k], 0, tops - 1)].astype(BF16)
        field = field + dot(found, top_ref[k], (1, 1))
    fields = [field]
    for level in reversed(range(levels)):
        first = 2 * subs - 2 * (subs >> level)
        fields = [
            dot(fields[j // 2].astype(BF16), level_ref[first + j], (1, 1)) for j in range(subs >> level)
        ]
    for j in range(subs):
        down_out[j] = fields[j].astype(kind)
    down_copies = deal(down_out, down_in, down_send, down_recv)

    @pl.loop(1 + 2 * third, leaves - 1)
    def _(leaf):
        inner(leaf)

    for side in range(2):
        @pl.when(sends[1 - side])
        def _():
            for n in range(3):
                halo_copy(side, n).wait_recv()

    def halo(side):
        return sides(halo_feat[side].astype(F32))[1], True, halo_vals[side]

    near(0, halo(0), own(1))
    near(leaves - 1, own(leaves - 2), halo(1))

    for copy in along[1:] + passed + to_mate[1:]:
        copy.wait_recv()
    pair_field = jnp.zeros((rank, columns), F32)
    for k in range(pair_list.shape[1]):
        source = nodes[jnp.clip(pair_list[0, k] - top * subs, 0, subs - 1)]
        term = dot(pair_ref[k], source, (1, 0))
        pair_field = pair_field + jnp.where(k < pair_count[0], term, 0.0)

    for copy in down_copies:
        copy.wait_recv()
    turned = jnp.concatenate([down_in[j].astype(F32) for j in range(subs)], axis=0)
    field = (turned.T + pair_field).astype(BF16)
    field_ref[...] = field
    field_copy = pltpu.make_async_copy(field_ref, field_hbm, field_sem)
    field_copy.start()

    twice_copy.wait()
    field_copy.wait()
    for leaf in range(leaves):
        near_copy(leaf).wait()
    for copy in along + to_mate + passed + part_copies + top_copies + down_copies:
        copy.wait_send()
    for side in range(2):
        @pl.when(sends[side])
        def _():
            for n in range(3):
                halo_copy(side, n).wait_send()


def scatter_kernel(
    twice_hbm, near_hbm, basis_hbm, transfer_hbm, field_hbm, out_hbm,
    twice_ref, near_ref, basis_ref, transfer_ref, field_ref, out_ref, leaf_field, mixed,
    load_sem, near_sem, basis_sem, out_sem,
):
    leaves, rows, rank = basis_ref.shape
    lanes = out_ref.shape[1]
    loads = [
        pltpu.make_async_copy(src, dst, load_sem.at[n])
        for n, (src, dst) in enumerate((
            (field_hbm, field_ref), (transfer_hbm, transfer_ref), (twice_hbm, twice_ref),
        ))
    ]

    def leaf_loads(leaf):
        return (
            pltpu.make_async_copy(near_hbm.at[leaf], near_ref.at[leaf], near_sem.at[leaf]),
            pltpu.make_async_copy(basis_hbm.at[leaf], basis_ref.at[leaf], basis_sem.at[leaf]),
        )

    for load in loads:
        load.start()
    for load in leaf_loads(0):
        load.start()
    for load in loads[:2]:
        load.wait()
    for leaf in range(1, leaves):
        for load in leaf_loads(leaf):
            load.start()
    for leaf in range(leaves):
        leaf_field[leaf] = dot(transfer_ref[leaf], field_ref[...], (1, 0)).astype(BF16)
    loads[2].wait()
    step = SLICES * DEPTH

    @pl.loop(0, leaves)
    def _(leaf):
        for load in leaf_loads(leaf):
            load.wait()
        total = near_ref[leaf] + dot(basis_ref[leaf], leaf_field[leaf], (1, 0))
        mixed[pl.ds(0, rows, stride=2), :] = total[:, :lanes]
        mixed[pl.ds(1, rows, stride=2), :] = total[:, lanes:]

        @pl.loop(0, rows // step)
        def _(i):
            bases = [i * step + q * DEPTH for q in range(SLICES)]
            places = [twice_ref.at[pl.ds(leaf * rows + base, DEPTH)] for base in bases]
            sources = [mixed.at[pl.ds(base * 2, DEPTH * 2)] for base in bases]
            for k in range(DEPTH):
                taken = [source[pl.ds(2 * k, 2), :] for source in sources]
                for place, rows_of in zip(places, taken):
                    out_ref[pl.ds(place[k], 2), :] = rows_of

    parts = out_sem.shape[0]
    size = out_ref.shape[0] // parts
    stores = [
        pltpu.make_async_copy(out_ref.at[pl.ds(n * size, size)], out_hbm.at[pl.ds(n * size, size)], out_sem.at[n])
        for n in range(parts)
    ]
    for store in stores:
        store.start()
    for store in stores:
        store.wait()


def per_device(
    subs, tops,
    points, vectors, inv_length, order, leaf_basis, leaf_transfer, level_transfer,
    near_list, near_count, pair_list, pair_count, pair_coupling, top_list, top_coupling,
):
    leaves, rows, rank = leaf_basis.shape
    count, features = points.shape
    lanes = vectors.shape[2]
    columns = vectors.shape[1] * lanes
    width = columns // subs
    kind = BF16 if width % 16 == 0 else F32
    order_flat = order.reshape(-1)

    operands = (
        order_flat, order_flat.reshape(-1, LANES), near_list.T, near_count, pair_list, pair_count, top_list,
        vectors, points.T, inv_length[None, :],
        leaf_basis, leaf_transfer, level_transfer[0], pair_coupling[0], top_coupling[0],
    )
    near_sum, field, twice = pl.pallas_call(
        functools.partial(near_kernel, subs, tops),
        name="near",
        out_shape=(
            jax.ShapeDtypeStruct((leaves, rows, columns), F32),
            jax.ShapeDtypeStruct((rank, columns), BF16),
            jax.ShapeDtypeStruct((count // LANES, LANES), jnp.int32),
        ),
        in_specs=[pl.BlockSpec(memory_space=pltpu.HBM)] * len(operands),
        out_specs=[pl.BlockSpec(memory_space=pltpu.HBM)] * 3,
        scratch_shapes=[
            *(pltpu.SMEM(v.shape, v.dtype) for v in (operands[0], *operands[2:7])),
            *(pltpu.VMEM(v.shape, v.dtype) for v in operands[7:]),
            pltpu.SemaphoreType.DMA((len(operands),)),
            pltpu.VMEM((leaves, rows, columns), F32),
            pltpu.SemaphoreType.DMA((leaves,)),
            pltpu.VMEM((rank, columns), BF16),
            pltpu.VMEM((count // LANES, LANES), jnp.int32),
            pltpu.SemaphoreType.DMA,
            pltpu.VMEM((count, 2, LANES), BF16),
            pltpu.VMEM((rows, 2, LANES), BF16),
            pltpu.VMEM((leaves, rows, columns), BF16),
            pltpu.VMEM((leaves, rows, 2 * LANES), BF16),
            pltpu.VMEM((2, features, rows), BF16),
            pltpu.VMEM((rank, columns), F32),
            pltpu.VMEM((rank, columns), BF16),
            pltpu.VMEM((2, features, rows), BF16),
            pltpu.VMEM((2, rows, columns), BF16),
            pltpu.VMEM((subs, rank, columns), BF16),
            pltpu.VMEM((subs, width, rank), kind),
            pltpu.VMEM((subs, width, rank), kind),
            pltpu.VMEM((width, rank), kind),
            pltpu.VMEM((tops, width, rank), kind),
            pltpu.VMEM((subs, width, rank), kind),
            pltpu.VMEM((subs, width, rank), kind),
            pltpu.SemaphoreType.DMA((subs - 1,)),
            pltpu.SemaphoreType.DMA((subs - 1,)),
            pltpu.SemaphoreType.DMA((subs - 1,)),
            pltpu.SemaphoreType.DMA((subs - 1,)),
            pltpu.SemaphoreType.DMA((subs // 2 - 2,)),
            pltpu.SemaphoreType.DMA((subs // 2 - 2,)),
            pltpu.SemaphoreType.DMA,
            pltpu.SemaphoreType.DMA((subs // 2 - 1,)),
            pltpu.SemaphoreType.DMA((subs // 2 - 1,)),
            pltpu.SemaphoreType.DMA((2,)),
            pltpu.SemaphoreType.DMA((2,)),
            pltpu.SemaphoreType.DMA((6,)),
            pltpu.SemaphoreType.DMA((6,)),
            pltpu.SemaphoreType.DMA((tops - 1,)),
            pltpu.SemaphoreType.DMA((tops - 1,)),
        ],
        compiler_params=pltpu.CompilerParams(
            collective_id=0, has_side_effects=True
        ),
    )(*operands)

    shares = (twice.reshape(-1), near_sum, leaf_basis, leaf_transfer, field)
    result = pl.pallas_call(
        scatter_kernel,
        name="scatter",
        out_shape=jax.ShapeDtypeStruct((count * 2, lanes), F32),
        in_specs=[pl.BlockSpec(memory_space=pltpu.HBM)] * len(shares),
        out_specs=pl.BlockSpec(memory_space=pltpu.HBM),
        scratch_shapes=[
            pltpu.SMEM((count,), jnp.int32),
            *(pltpu.VMEM(v.shape, v.dtype) for v in shares[1:]),
            pltpu.VMEM((count * 2, lanes), F32),
            pltpu.VMEM((leaves, rank, columns), BF16),
            pltpu.VMEM((rows * 2, lanes), F32),
            pltpu.SemaphoreType.DMA((3,)),
            pltpu.SemaphoreType.DMA((leaves,)),
            pltpu.SemaphoreType.DMA((leaves,)),
            pltpu.SemaphoreType.DMA((leaves,)),
        ],
    )(*shares)
    return result.reshape(count, vectors.shape[1], lanes)


def solution(mesh):
    shape = dict(mesh.shape)
    both = ("leaf", "sub")
    return jax.shard_map(
        functools.partial(per_device, shape["sub"], shape["leaf"]),
        mesh=mesh,
        in_specs=(
            P(both, None), P(both, None, None), P(), P(both, None), P(both, None, None),
            P(both, None, None), P("leaf", None, None, None), P(both, None), P(both),
            P(both, None), P(both), P(both, None, None, None), P("leaf", None),
            P("leaf", None, None, None),
        ),
        out_specs=P(both, None, None),
        check_vma=False,
    )
```

```python
import functools
import math

import jax
import jax.numpy as jnp
from jax import lax
from jax.experimental import pallas as pl
from jax.experimental.pallas import tpu as pltpu
from jax.sharding import PartitionSpec as P

MESH = pl.DeviceIdType.MESH
LOG2E = math.log2(math.e)
F32 = jnp.float32
BF16 = jnp.bfloat16
LANES = 128
SLICES = 8
DEPTH = 16
STEP = 512
REACH = 4


def dot(a, b, dims):
    return lax.dot_general(a, b, ((dims[:1], dims[1:]), ((), ())), preferred_element_type=F32)


def bf16_parts(value):
    high = value.astype(BF16).astype(F32)
    rest = value - high
    mid = rest.astype(BF16).astype(F32)
    low = (rest - mid).astype(BF16).astype(F32)
    return high, mid, low


def tile_of(lhs, rhs, turned):
    return jnp.exp2(dot(lhs, rhs, (1, 0 if turned else 1))).astype(BF16)


def sides(x):
    features, count = x.shape
    half = bf16_parts((-0.5 * LOG2E) * jnp.sum(x * x, axis=0, keepdims=True))
    ones = jnp.ones((3, count), F32)
    pad = jnp.zeros((2, count), F32)
    rest = jnp.zeros((LANES - 3 * features - 8, count), F32)
    left = jnp.concatenate([*bf16_parts(x * LOG2E), jnp.concatenate([*half, ones, pad], axis=0), rest], axis=0)
    right = jnp.concatenate([x, x, x, jnp.concatenate([ones, *half, pad], axis=0), rest], axis=0)
    return left.astype(BF16), right.astype(BF16)


def take_rows(order_ref, table, start, out):
    step = SLICES * DEPTH

    @pl.loop(0, out.shape[0] // step)
    def _(i):
        bases = [i * step + q * DEPTH for q in range(SLICES)]
        places = [order_ref.at[pl.ds(start + base, DEPTH)] for base in bases]
        targets = [out.at[pl.ds(base, DEPTH)] for base in bases]
        for k in range(DEPTH):
            for place, target in zip(places, targets):
                target[k] = table[place[k]]


def split_rows(got, out, leaf):
    flat = got.reshape(2 * got.shape[0], LANES)
    for half in range(2):
        out[leaf, :, half * LANES:(half + 1) * LANES] = flat[pl.ds(half, got.shape[0], stride=2), :]


def near_kernel(
    subs, tops,
    order_hbm, twice_src, list_hbm, count_hbm, pairs_hbm, used_hbm, tops_hbm,
    vec_hbm, pts_hbm, inv_hbm, basis_hbm, transfer_hbm, level_hbm, pair_hbm, top_hbm,
    near_hbm, field_hbm, twice_hbm,
    order_ref, near_list, near_count, pair_list, pair_count, top_list,
    vec_ref, pts_ref, inv_ref, basis_ref, transfer_ref, level_ref, pair_ref, top_ref,
    load_sem, near_ref, near_sem,
    field_ref, order_vec, twice_sem, table, got, ordered, feat, edge_feat, node_sum, node_low,
    halo_feat, halo_vals, nodes, part_out, part_in, top_low, top_all, down_out, down_in,
    part_send, part_recv, down_send, down_recv, fore_send, fore_recv, field_sem,
    node_send, node_recv, pass_send, pass_recv, halo_send, halo_recv, top_send, top_recv,
):
    leaves, rows, rank = basis_ref.shape
    features, count = pts_ref.shape
    columns = ordered.shape[2]
    sub = lax.axis_index("sub")
    top = lax.axis_index("leaf")
    levels = subs.bit_length() - 1
    first_leaf = (top * subs + sub) * leaves
    mate = sub + 1 - 2 * lax.rem(sub, 2)

    loads = [
        pltpu.make_async_copy(src, dst, load_sem.at[n])
        for n, (src, dst) in enumerate((
            (vec_hbm, vec_ref), (order_hbm, order_ref), (basis_hbm, basis_ref),
            (transfer_hbm, transfer_ref), (pts_hbm, pts_ref), (inv_hbm, inv_ref),
            (twice_src, order_vec), (level_hbm, level_ref),
            (pair_hbm, pair_ref), (top_hbm, top_ref), (list_hbm, near_list),
            (count_hbm, near_count), (pairs_hbm, pair_list), (used_hbm, pair_count),
            (tops_hbm, top_list),
        ))
    ]
    for load in loads:
        load.start()

    nodes[...] = jnp.zeros(nodes.shape, BF16)
    barrier = pltpu.get_barrier_semaphore()
    for d in range(1, subs):
        pl.semaphore_signal(barrier, inc=1, device_id={"sub": lax.rem(sub + d, subs)}, device_id_type=MESH)
    for d in range(1, tops):
        pl.semaphore_signal(barrier, inc=1, device_id={"leaf": lax.rem(top + d, tops)}, device_id_type=MESH)

    def fetch(leaf):
        take_rows(order_ref, vec_ref, leaf * rows, got)
        split_rows(got, ordered, leaf)

    def lift(leaf):
        coef = dot(basis_ref[leaf], ordered[leaf], (0, 0)).astype(BF16)
        node_sum[...] = node_sum[...] + dot(transfer_ref[leaf], coef, (0, 0))

    node_sum[...] = jnp.zeros_like(node_sum)
    for load in loads[:2]:
        load.wait()
    fetch(leaves - 1)
    fetch(0)
    for load in loads[2:4]:
        load.wait()
    lift(leaves - 1)
    lift(0)

    @pl.loop(1, leaves // 2 - 1)
    def _(leaf):
        fetch(leaf)
        lift(leaf)

    pl.semaphore_wait(barrier, subs + tops - 2)

    def halo_copy(side, n):
        leaf, peer = (leaves - 1, sub + 1) if side == 0 else (0, sub - 1)
        part = (pl.ds(0, rows // 4), pl.ds(rows // 4, rows - rows // 4))[n % 2]
        src, dst = (
            (ordered.at[leaf, part], halo_vals.at[side, part]),
            (ordered.at[leaf, part], halo_vals.at[side, part]),
            (edge_feat.at[side], halo_feat.at[side]),
        )[n]
        return pltpu.make_async_remote_copy(
            src_ref=src, dst_ref=dst,
            send_sem=halo_send.at[3 * side + n], recv_sem=halo_recv.at[3 * side + n],
            device_id={"sub": jnp.clip(peer, 0, subs - 1)}, device_id_type=MESH,
        )

    sends = (sub < subs - 1, sub > 0)
    for side in range(2):
        @pl.when(sends[side])
        def _():
            halo_copy(side, 0).start()

        @pl.when(jnp.logical_not(sends[1 - side]))
        def _():
            halo_feat[side] = jnp.zeros(halo_feat.shape[1:], BF16)
            halo_vals[side] = jnp.zeros(halo_vals.shape[1:], BF16)

    @pl.loop(leaves // 2 - 1, leaves - 1)
    def _(leaf):
        fetch(leaf)
        lift(leaf)

    node = node_sum[...].astype(BF16)
    node_low[...] = node
    nodes[sub] = node

    for load in loads[4:]:
        load.wait()

    width = columns // subs
    kind = part_out.dtype
    raised = dot(node, level_ref[sub], (0, 0))
    for level in range(1, levels):
        place = 2 * subs - 2 * (subs >> level) + jnp.right_shift(sub, level)
        raised = dot(raised.astype(BF16), level_ref[place], (1, 0))
    for j in range(subs):
        part_out[j] = raised[j * width:(j + 1) * width].astype(kind)

    def deal(source, target, sends_to, recvs):
        copies = []
        for d in range(1, subs):
            peer = lax.rem(sub + d, subs)
            copies.append(pltpu.make_async_remote_copy(
                src_ref=source.at[peer], dst_ref=target.at[sub],
                send_sem=sends_to.at[d - 1], recv_sem=recvs.at[d - 1],
                device_id={"sub": peer}, device_id_type=MESH,
            ))
        for copy in copies:
            copy.start()
        target[sub] = source[sub]
        return copies

    part_copies = deal(part_out, part_in, part_send, part_recv)

    def node_copy(n, src, dst, peer, sends_to, recvs):
        return pltpu.make_async_remote_copy(
            src_ref=src, dst_ref=dst, send_sem=sends_to.at[n], recv_sem=recvs.at[n],
            device_id={"sub": peer}, device_id_type=MESH,
        )

    def within(place):
        return (place >= 0) & (place < subs)

    def inside(place):
        return jnp.clip(place, 0, subs - 1)

    far = tuple(d for step in range(REACH, 0, -2) for d in (step, -step))
    parity = lax.rem(sub, 2)

    def along(n):
        return node_copy(n, node_low, nodes.at[sub], inside(sub + far[n]), node_send, node_recv)

    def forward(n):
        return node_copy(n, nodes.at[mate], nodes.at[mate], inside(sub + far[2 + n]), fore_send, fore_recv)

    def relay():
        origin = inside(sub + REACH - 2 * REACH * parity)
        return node_copy(1, nodes.at[origin], nodes.at[origin], mate, pass_send, pass_recv)

    relays = within(sub + REACH - 2 * REACH * parity)
    relayed = within(mate - REACH + 2 * REACH * parity)

    def each(make, spans, act):
        for n, span in enumerate(spans):
            @pl.when(within(sub + span))
            def _():
                act(make(n))

    to_mate = node_copy(0, node_low, nodes.at[sub], mate, pass_send, pass_recv)
    to_mate.start()
    each(along, far, lambda copy: copy.start())
    for side in range(2):
        @pl.when(sends[side])
        def _():
            halo_copy(side, 1).start()

    order_vec[...] = order_vec[...] * 2
    twice_copy = pltpu.make_async_copy(order_vec, twice_hbm, twice_sem)
    twice_copy.start()

    square = (features, features)
    same = lax.broadcasted_iota(jnp.int32, square, 0) == lax.broadcasted_iota(jnp.int32, square, 1)
    inv = jnp.sum(jnp.where(same, jnp.broadcast_to(inv_ref[...], square), 0.0), axis=1, keepdims=True)

    @pl.loop(0, count // STEP)
    def _(i):
        for part in range(STEP // LANES):
            start = pl.multiple_of(i * STEP + part * LANES, LANES)
            x = (pts_ref[:, pl.ds(start, LANES)].astype(F32) * inv).astype(BF16).astype(F32)
            both = jnp.concatenate(sides(x), axis=0).T
            table[pl.ds(start, LANES)] = both.reshape(LANES, 2, LANES)

    def features_of(leaf):
        take_rows(order_ref, table, leaf * rows, got)
        split_rows(got, feat, leaf)

    for side, leaf in ((0, leaves - 1), (1, 0)):
        features_of(leaf)
        edge_feat[side] = feat[leaf][:, LANES:].T[:features]

        @pl.when(sends[side])
        def _():
            halo_copy(side, 2).start()

    @pl.loop(1, leaves // 2)
    def _(leaf):
        features_of(leaf)

    @pl.loop(leaves // 2, leaves - 1)
    def _(leaf):
        features_of(leaf)

    def wanted(leaf, target):
        found = jnp.int32(0)
        for k in range(near_list.shape[0]):
            found = found | ((near_list[k, leaf] == target) & (k < near_count[leaf])).astype(jnp.int32)
        return found.astype(F32).astype(BF16)

    def near_copy(leaf):
        return pltpu.make_async_copy(near_ref.at[leaf], near_hbm.at[leaf], near_sem.at[leaf])

    def near(leaf, before, after):
        flag_before = wanted(leaf, first_leaf + leaf - 1)
        flag_after = wanted(leaf, first_leaf + leaf + 1)
        tiles, values = [], []
        for (rhs, turned, vals), flag in (
            ((feat[leaf][:, LANES:], False, ordered[leaf]), None),
            (before, flag_before),
            (after, flag_after),
        ):
            tiles.append(tile_of(feat[leaf][:, :LANES], rhs, turned))
            values.append(vals if flag is None else vals * flag)
        near_ref[leaf] = dot(jnp.concatenate(tiles, axis=1), jnp.concatenate(values, axis=0), (1, 0))
        near_copy(leaf).start()

    def own(leaf):
        return feat[leaf][:, LANES:], False, ordered[leaf]

    def inner(leaf):
        near(leaf, own(leaf - 1), own(leaf + 1))

    to_mate.wait_recv()
    each(forward, far[2:], lambda copy: copy.start())

    @pl.loop(1, 2)
    def _(leaf):
        inner(leaf)

    for copy in part_copies:
        copy.wait_recv()
    root = part_in[0].astype(F32)
    for j in range(1, subs):
        root = root + part_in[j].astype(F32)
    root = root.astype(BF16).astype(kind)
    top_low[...] = root
    top_all[top] = root
    top_copies = []
    for d in range(1, tops):
        copy = pltpu.make_async_remote_copy(
            src_ref=top_low, dst_ref=top_all.at[top],
            send_sem=top_send.at[d - 1], recv_sem=top_recv.at[d - 1],
            device_id={"leaf": lax.rem(top + d, tops)}, device_id_type=MESH,
        )
        copy.start()
        top_copies.append(copy)

    for n in range(2):
        @pl.when(within(sub - far[n]))
        def _():
            along(n).wait_recv()

    @pl.when(relays)
    def _():
        relay().start()

    @pl.loop(2, 4)
    def _(leaf):
        inner(leaf)

    for copy in top_copies:
        copy.wait_recv()
    field = jnp.zeros((width, rank), F32)
    for k in range(top_list.shape[1]):
        found = top_all[jnp.clip(top_list[0, k], 0, tops - 1)].astype(BF16)
        field = field + dot(found, top_ref[k], (1, 1))
    fields = [field]
    for level in reversed(range(levels)):
        first = 2 * subs - 2 * (subs >> level)
        fields = [
            dot(fields[j // 2].astype(BF16), level_ref[first + j], (1, 1)) for j in range(subs >> level)
        ]
    for j in range(subs):
        down_out[j] = fields[j].astype(kind)
    down_copies = deal(down_out, down_in, down_send, down_recv)

    @pl.loop(4, leaves - 1)
    def _(leaf):
        inner(leaf)

    for side in range(2):
        @pl.when(sends[1 - side])
        def _():
            for n in range(3):
                halo_copy(side, n).wait_recv()

    def halo(side):
        return sides(halo_feat[side].astype(F32))[1], True, halo_vals[side]

    near(0, halo(0), own(1))
    near(leaves - 1, own(leaves - 2), halo(1))

    for n in range(2, len(far)):
        @pl.when(within(sub - far[n]))
        def _():
            along(n).wait_recv()
            forward(n - 2).wait_recv()

    @pl.when(relayed)
    def _():
        relay().wait_recv()

    pair_field = jnp.zeros((rank, columns), F32)
    for k in range(pair_list.shape[1]):
        source = nodes[jnp.clip(pair_list[0, k] - top * subs, 0, subs - 1)]
        term = dot(pair_ref[k], source, (1, 0))
        pair_field = pair_field + jnp.where(k < pair_count[0], term, 0.0)

    for copy in down_copies:
        copy.wait_recv()
    turned = jnp.concatenate([down_in[j].astype(F32) for j in range(subs)], axis=0)
    field = (turned.T + pair_field).astype(BF16)
    field_ref[...] = field
    field_copy = pltpu.make_async_copy(field_ref, field_hbm, field_sem)
    field_copy.start()

    twice_copy.wait()
    field_copy.wait()
    for leaf in range(leaves):
        near_copy(leaf).wait()
    each(along, far, lambda copy: copy.wait_send())
    each(forward, far[2:], lambda copy: copy.wait_send())

    @pl.when(relays)
    def _():
        relay().wait_send()

    for copy in [to_mate] + part_copies + top_copies + down_copies:
        copy.wait_send()
    for side in range(2):
        @pl.when(sends[side])
        def _():
            for n in range(3):
                halo_copy(side, n).wait_send()


def scatter_kernel(
    twice_hbm, near_hbm, basis_hbm, transfer_hbm, field_hbm, out_hbm,
    twice_ref, near_ref, basis_ref, transfer_ref, field_ref, out_ref, leaf_field, even, odd,
    load_sem, near_sem, basis_sem, out_sem,
):
    leaves, rows, rank = basis_ref.shape
    lanes = out_ref.shape[1]
    loads = [
        pltpu.make_async_copy(src, dst, load_sem.at[n])
        for n, (src, dst) in enumerate((
            (field_hbm, field_ref), (transfer_hbm, transfer_ref), (twice_hbm, twice_ref),
        ))
    ]

    def leaf_loads(leaf):
        return (
            pltpu.make_async_copy(near_hbm.at[leaf], near_ref.at[leaf], near_sem.at[leaf]),
            pltpu.make_async_copy(basis_hbm.at[leaf], basis_ref.at[leaf], basis_sem.at[leaf]),
        )

    for load in loads:
        load.start()
    for load in leaf_loads(0):
        load.start()
    for load in loads[:2]:
        load.wait()
    for leaf in range(1, leaves):
        for load in leaf_loads(leaf):
            load.start()
    for leaf in range(leaves):
        leaf_field[leaf] = dot(transfer_ref[leaf], field_ref[...], (1, 0)).astype(BF16)
    loads[2].wait()
    step = SLICES * DEPTH
    chunks = rows // step

    def fill(target, leaf, chunk):
        place = pl.ds(chunk * step, step)
        total = near_ref[leaf, place] + dot(basis_ref[leaf, place], leaf_field[leaf], (1, 0))
        target[pl.ds(0, step, stride=2), :] = total[:, :lanes]
        target[pl.ds(1, step, stride=2), :] = total[:, lanes:]

    def spread(source, leaf, chunk):
        bases = [q * DEPTH for q in range(SLICES)]
        places = [twice_ref.at[pl.ds(leaf * rows + chunk * step + base, DEPTH)] for base in bases]
        for k in range(DEPTH):
            taken = [source[pl.ds(2 * (base + k), 2), :] for base in bases]
            for place, rows_of in zip(places, taken):
                out_ref[pl.ds(place[k], 2), :] = rows_of

    def emit(leaf, last):
        for chunk in range(chunks):
            if chunk + 1 < chunks:
                fill(mixed[(chunk + 1) % 2], leaf, chunk + 1)
            elif not last:
                fill(mixed[0], leaf + 1, 0)
            spread(mixed[chunk % 2], leaf, chunk)

    mixed = (even, odd)
    for load in leaf_loads(0):
        load.wait()
    fill(even, 0, 0)

    @pl.loop(0, leaves - 1)
    def _(leaf):
        for load in leaf_loads(leaf + 1):
            load.wait()
        emit(leaf, False)

    emit(leaves - 1, True)

    parts = out_sem.shape[0]
    size = out_ref.shape[0] // parts
    stores = [
        pltpu.make_async_copy(out_ref.at[pl.ds(n * size, size)], out_hbm.at[pl.ds(n * size, size)], out_sem.at[n])
        for n in range(parts)
    ]
    for store in stores:
        store.start()
    for store in stores:
        store.wait()


def per_device(
    subs, tops,
    points, vectors, inv_length, order, leaf_basis, leaf_transfer, level_transfer,
    near_list, near_count, pair_list, pair_count, pair_coupling, top_list, top_coupling,
):
    leaves, rows, rank = leaf_basis.shape
    count, features = points.shape
    lanes = vectors.shape[2]
    columns = vectors.shape[1] * lanes
    width = columns // subs
    kind = BF16 if width % 16 == 0 else F32
    order_flat = order.reshape(-1)

    operands = (
        order_flat, order_flat.reshape(-1, LANES), near_list.T, near_count, pair_list, pair_count, top_list,
        vectors, points.T, inv_length[None, :],
        leaf_basis, leaf_transfer, level_transfer[0], pair_coupling[0], top_coupling[0],
    )
    near_sum, field, twice = pl.pallas_call(
        functools.partial(near_kernel, subs, tops),
        name="near",
        out_shape=(
            jax.ShapeDtypeStruct((leaves, rows, columns), F32),
            jax.ShapeDtypeStruct((rank, columns), BF16),
            jax.ShapeDtypeStruct((count // LANES, LANES), jnp.int32),
        ),
        in_specs=[pl.BlockSpec(memory_space=pltpu.HBM)] * len(operands),
        out_specs=[pl.BlockSpec(memory_space=pltpu.HBM)] * 3,
        scratch_shapes=[
            *(pltpu.SMEM(v.shape, v.dtype) for v in (operands[0], *operands[2:7])),
            *(pltpu.VMEM(v.shape, v.dtype) for v in operands[7:]),
            pltpu.SemaphoreType.DMA((len(operands),)),
            pltpu.VMEM((leaves, rows, columns), F32),
            pltpu.SemaphoreType.DMA((leaves,)),
            pltpu.VMEM((rank, columns), BF16),
            pltpu.VMEM((count // LANES, LANES), jnp.int32),
            pltpu.SemaphoreType.DMA,
            pltpu.VMEM((count, 2, LANES), BF16),
            pltpu.VMEM((rows, 2, LANES), BF16),
            pltpu.VMEM((leaves, rows, columns), BF16),
            pltpu.VMEM((leaves, rows, 2 * LANES), BF16),
            pltpu.VMEM((2, features, rows), BF16),
            pltpu.VMEM((rank, columns), F32),
            pltpu.VMEM((rank, columns), BF16),
            pltpu.VMEM((2, features, rows), BF16),
            pltpu.VMEM((2, rows, columns), BF16),
            pltpu.VMEM((subs, rank, columns), BF16),
            pltpu.VMEM((subs, width, rank), kind),
            pltpu.VMEM((subs, width, rank), kind),
            pltpu.VMEM((width, rank), kind),
            pltpu.VMEM((tops, width, rank), kind),
            pltpu.VMEM((subs, width, rank), kind),
            pltpu.VMEM((subs, width, rank), kind),
            pltpu.SemaphoreType.DMA((subs - 1,)),
            pltpu.SemaphoreType.DMA((subs - 1,)),
            pltpu.SemaphoreType.DMA((subs - 1,)),
            pltpu.SemaphoreType.DMA((subs - 1,)),
            pltpu.SemaphoreType.DMA((REACH - 2,)),
            pltpu.SemaphoreType.DMA((REACH - 2,)),
            pltpu.SemaphoreType.DMA,
            pltpu.SemaphoreType.DMA((REACH,)),
            pltpu.SemaphoreType.DMA((REACH,)),
            pltpu.SemaphoreType.DMA((2,)),
            pltpu.SemaphoreType.DMA((2,)),
            pltpu.SemaphoreType.DMA((6,)),
            pltpu.SemaphoreType.DMA((6,)),
            pltpu.SemaphoreType.DMA((tops - 1,)),
            pltpu.SemaphoreType.DMA((tops - 1,)),
        ],
        compiler_params=pltpu.CompilerParams(
            collective_id=0, has_side_effects=True
        ),
    )(*operands)

    shares = (twice.reshape(-1), near_sum, leaf_basis, leaf_transfer, field)
    result = pl.pallas_call(
        scatter_kernel,
        name="scatter",
        out_shape=jax.ShapeDtypeStruct((count * 2, lanes), F32),
        in_specs=[pl.BlockSpec(memory_space=pltpu.HBM)] * len(shares),
        out_specs=pl.BlockSpec(memory_space=pltpu.HBM),
        scratch_shapes=[
            pltpu.SMEM((count,), jnp.int32),
            *(pltpu.VMEM(v.shape, v.dtype) for v in shares[1:]),
            pltpu.VMEM((count * 2, lanes), F32),
            pltpu.VMEM((leaves, rank, columns), BF16),
            pltpu.VMEM((SLICES * DEPTH * 2, lanes), F32),
            pltpu.VMEM((SLICES * DEPTH * 2, lanes), F32),
            pltpu.SemaphoreType.DMA((3,)),
            pltpu.SemaphoreType.DMA((leaves,)),
            pltpu.SemaphoreType.DMA((leaves,)),
            pltpu.SemaphoreType.DMA((leaves,)),
        ],
    )(*shares)
    return result.reshape(count, vectors.shape[1], lanes)


def solution(mesh):
    shape = dict(mesh.shape)
    both = ("leaf", "sub")
    return jax.shard_map(
        functools.partial(per_device, shape["sub"], shape["leaf"]),
        mesh=mesh,
        in_specs=(
            P(both, None), P(both, None, None), P(), P(both, None), P(both, None, None),
            P(both, None, None), P("leaf", None, None, None), P(both, None), P(both),
            P(both, None), P(both), P(both, None, None, None), P("leaf", None),
            P("leaf", None, None, None),
        ),
        out_specs=P(both, None, None),
        check_vma=False,
    )
```

```python
import functools
import math

import jax
import jax.numpy as jnp
from jax import lax
from jax.experimental import pallas as pl
from jax.experimental.pallas import tpu as pltpu
from jax.sharding import PartitionSpec as P

MESH = pl.DeviceIdType.MESH
LOG2E = math.log2(math.e)
F32 = jnp.float32
BF16 = jnp.bfloat16
LANES = 128
SLICES = 8
DEPTH = 16
STEP = 512
REACH = 4


def dot(a, b, dims):
    return lax.dot_general(a, b, ((dims[:1], dims[1:]), ((), ())), preferred_element_type=F32)


def bf16_parts(value):
    high = value.astype(BF16).astype(F32)
    rest = value - high
    mid = rest.astype(BF16).astype(F32)
    low = (rest - mid).astype(BF16).astype(F32)
    return high, mid, low


def tile_of(lhs, rhs, turned):
    return jnp.exp2(dot(lhs, rhs, (1, 0 if turned else 1))).astype(BF16)


def sides(x):
    features, count = x.shape
    half = bf16_parts((-0.5 * LOG2E) * jnp.sum(x * x, axis=0, keepdims=True))
    ones = jnp.ones((3, count), F32)
    pad = jnp.zeros((2, count), F32)
    rest = jnp.zeros((LANES - 3 * features - 8, count), F32)
    left = jnp.concatenate([*bf16_parts(x * LOG2E), jnp.concatenate([*half, ones, pad], axis=0), rest], axis=0)
    right = jnp.concatenate([x, x, x, jnp.concatenate([ones, *half, pad], axis=0), rest], axis=0)
    return left.astype(BF16), right.astype(BF16)


def take_rows(order_ref, table, start, out):
    step = SLICES * DEPTH

    @pl.loop(0, out.shape[0] // step)
    def _(i):
        bases = [i * step + q * DEPTH for q in range(SLICES)]
        places = [order_ref.at[pl.ds(start + base, DEPTH)] for base in bases]
        targets = [out.at[pl.ds(base, DEPTH)] for base in bases]
        for k in range(DEPTH):
            for place, target in zip(places, targets):
                target[k] = table[place[k]]


def split_rows(got, out, leaf):
    flat = got.reshape(2 * got.shape[0], LANES)
    for half in range(2):
        out[leaf, :, half * LANES:(half + 1) * LANES] = flat[pl.ds(half, got.shape[0], stride=2), :]


def near_kernel(
    subs, tops,
    order_hbm, twice_src, list_hbm, count_hbm, pairs_hbm, used_hbm, tops_hbm,
    vec_hbm, pts_hbm, inv_hbm, basis_hbm, transfer_hbm, level_hbm, pair_hbm, top_hbm,
    near_hbm, field_hbm, twice_hbm,
    order_ref, near_list, near_count, pair_list, pair_count, top_list,
    vec_ref, pts_ref, inv_ref, basis_ref, transfer_ref, level_ref, pair_ref, top_ref,
    load_sem, near_ref, near_sem,
    field_ref, order_vec, twice_sem, table, got, ordered, feat, edge_feat, node_sum, node_low,
    halo_feat, halo_vals, nodes, part_out, part_in, top_low, top_all, down_out, down_in,
    part_send, part_recv, down_send, down_recv, fore_send, fore_recv, field_sem,
    node_send, node_recv, pass_send, pass_recv, halo_send, halo_recv, top_send, top_recv,
):
    leaves, rows, rank = basis_ref.shape
    features, count = pts_ref.shape
    columns = ordered.shape[2]
    sub = lax.axis_index("sub")
    top = lax.axis_index("leaf")
    levels = subs.bit_length() - 1
    first_leaf = (top * subs + sub) * leaves
    mate = sub + 1 - 2 * lax.rem(sub, 2)

    loads = [
        pltpu.make_async_copy(src, dst, load_sem.at[n])
        for n, (src, dst) in enumerate((
            (vec_hbm, vec_ref), (order_hbm, order_ref), (basis_hbm, basis_ref),
            (transfer_hbm, transfer_ref), (pts_hbm, pts_ref), (inv_hbm, inv_ref),
            (twice_src, order_vec), (level_hbm, level_ref),
            (pair_hbm, pair_ref), (top_hbm, top_ref), (list_hbm, near_list),
            (count_hbm, near_count), (pairs_hbm, pair_list), (used_hbm, pair_count),
            (tops_hbm, top_list),
        ))
    ]
    for load in loads:
        load.start()

    nodes[...] = jnp.zeros(nodes.shape, BF16)
    barrier = pltpu.get_barrier_semaphore()
    for d in range(1, subs):
        pl.semaphore_signal(barrier, inc=1, device_id={"sub": lax.rem(sub + d, subs)}, device_id_type=MESH)
    for d in range(1, tops):
        pl.semaphore_signal(barrier, inc=1, device_id={"leaf": lax.rem(top + d, tops)}, device_id_type=MESH)

    def fetch(leaf):
        take_rows(order_ref, vec_ref, leaf * rows, got)
        split_rows(got, ordered, leaf)

    def lift(leaf):
        coef = dot(basis_ref[leaf], ordered[leaf], (0, 0)).astype(BF16)
        node_sum[...] = node_sum[...] + dot(transfer_ref[leaf], coef, (0, 0))

    node_sum[...] = jnp.zeros_like(node_sum)
    for load in loads[:2]:
        load.wait()
    fetch(leaves - 1)
    fetch(0)
    for load in loads[2:4]:
        load.wait()
    lift(leaves - 1)
    lift(0)

    @pl.loop(1, 2)
    def _(leaf):
        fetch(leaf)
        lift(leaf)

    pl.semaphore_wait(barrier, subs + tops - 2)

    def halo_copy(side, n):
        leaf, peer = (leaves - 1, sub + 1) if side == 0 else (0, sub - 1)
        part = (pl.ds(0, rows // 4), pl.ds(rows // 4, rows - rows // 4))[n % 2]
        src, dst = (
            (ordered.at[leaf, part], halo_vals.at[side, part]),
            (ordered.at[leaf, part], halo_vals.at[side, part]),
            (edge_feat.at[side], halo_feat.at[side]),
        )[n]
        return pltpu.make_async_remote_copy(
            src_ref=src, dst_ref=dst,
            send_sem=halo_send.at[3 * side + n], recv_sem=halo_recv.at[3 * side + n],
            device_id={"sub": jnp.clip(peer, 0, subs - 1)}, device_id_type=MESH,
        )

    sends = (sub < subs - 1, sub > 0)
    for side in range(2):
        @pl.when(sends[side])
        def _():
            halo_copy(side, 0).start()

        @pl.when(jnp.logical_not(sends[1 - side]))
        def _():
            halo_feat[side] = jnp.zeros(halo_feat.shape[1:], BF16)
            halo_vals[side] = jnp.zeros(halo_vals.shape[1:], BF16)

    @pl.loop(2, leaves - 1)
    def _(leaf):
        fetch(leaf)
        lift(leaf)

    node = node_sum[...].astype(BF16)
    node_low[...] = node
    nodes[sub] = node

    for load in loads[4:]:
        load.wait()

    width = columns // subs
    kind = part_out.dtype
    raised = dot(node, level_ref[sub], (0, 0))
    for level in range(1, levels):
        place = 2 * subs - 2 * (subs >> level) + jnp.right_shift(sub, level)
        raised = dot(raised.astype(BF16), level_ref[place], (1, 0))
    for j in range(subs):
        part_out[j] = raised[j * width:(j + 1) * width].astype(kind)

    def deal(source, target, sends_to, recvs):
        copies = []
        for d in range(1, subs):
            peer = lax.rem(sub + d, subs)
            copies.append(pltpu.make_async_remote_copy(
                src_ref=source.at[peer], dst_ref=target.at[sub],
                send_sem=sends_to.at[d - 1], recv_sem=recvs.at[d - 1],
                device_id={"sub": peer}, device_id_type=MESH,
            ))
        for copy in copies:
            copy.start()
        target[sub] = source[sub]
        return copies

    part_copies = deal(part_out, part_in, part_send, part_recv)

    def node_copy(n, src, dst, peer, sends_to, recvs):
        return pltpu.make_async_remote_copy(
            src_ref=src, dst_ref=dst, send_sem=sends_to.at[n], recv_sem=recvs.at[n],
            device_id={"sub": peer}, device_id_type=MESH,
        )

    def within(place):
        return (place >= 0) & (place < subs)

    def inside(place):
        return jnp.clip(place, 0, subs - 1)

    far = tuple(d for step in range(REACH, 0, -2) for d in (step, -step))
    parity = lax.rem(sub, 2)

    def along(n):
        return node_copy(n, node_low, nodes.at[sub], inside(sub + far[n]), node_send, node_recv)

    def forward(n):
        return node_copy(n, nodes.at[mate], nodes.at[mate], inside(sub + far[2 + n]), fore_send, fore_recv)

    def relay():
        origin = inside(sub + REACH - 2 * REACH * parity)
        return node_copy(1, nodes.at[origin], nodes.at[origin], mate, pass_send, pass_recv)

    relays = within(sub + REACH - 2 * REACH * parity)
    relayed = within(mate - REACH + 2 * REACH * parity)

    def each(make, spans, act):
        for n, span in enumerate(spans):
            @pl.when(within(sub + span))
            def _():
                act(make(n))

    to_mate = node_copy(0, node_low, nodes.at[sub], mate, pass_send, pass_recv)
    to_mate.start()
    each(along, far, lambda copy: copy.start())
    for side in range(2):
        @pl.when(sends[side])
        def _():
            halo_copy(side, 1).start()

    order_vec[...] = order_vec[...] * 2
    twice_copy = pltpu.make_async_copy(order_vec, twice_hbm, twice_sem)
    twice_copy.start()

    square = (features, features)
    same = lax.broadcasted_iota(jnp.int32, square, 0) == lax.broadcasted_iota(jnp.int32, square, 1)
    inv = jnp.sum(jnp.where(same, jnp.broadcast_to(inv_ref[...], square), 0.0), axis=1, keepdims=True)

    @pl.loop(0, count // STEP)
    def _(i):
        for part in range(STEP // LANES):
            start = pl.multiple_of(i * STEP + part * LANES, LANES)
            x = (pts_ref[:, pl.ds(start, LANES)].astype(F32) * inv).astype(BF16).astype(F32)
            both = jnp.concatenate(sides(x), axis=0).T
            table[pl.ds(start, LANES)] = both.reshape(LANES, 2, LANES)

    def features_of(leaf):
        take_rows(order_ref, table, leaf * rows, got)
        split_rows(got, feat, leaf)

    for side, leaf in ((0, leaves - 1), (1, 0)):
        features_of(leaf)
        edge_feat[side] = feat[leaf][:, LANES:].T[:features]

        @pl.when(sends[side])
        def _():
            halo_copy(side, 2).start()

    @pl.loop(1, leaves // 2)
    def _(leaf):
        features_of(leaf)

    @pl.loop(leaves // 2, leaves - 1)
    def _(leaf):
        features_of(leaf)

    def wanted(leaf, target):
        found = jnp.int32(0)
        for k in range(near_list.shape[0]):
            found = found | ((near_list[k, leaf] == target) & (k < near_count[leaf])).astype(jnp.int32)
        return found.astype(F32).astype(BF16)

    def near_copy(leaf):
        return pltpu.make_async_copy(near_ref.at[leaf], near_hbm.at[leaf], near_sem.at[leaf])

    def near(leaf, before, after):
        flag_before = wanted(leaf, first_leaf + leaf - 1)
        flag_after = wanted(leaf, first_leaf + leaf + 1)
        tiles, values = [], []
        for (rhs, turned, vals), flag in (
            ((feat[leaf][:, LANES:], False, ordered[leaf]), None),
            (before, flag_before),
            (after, flag_after),
        ):
            tiles.append(tile_of(feat[leaf][:, :LANES], rhs, turned))
            values.append(vals if flag is None else vals * flag)
        near_ref[leaf] = dot(jnp.concatenate(tiles, axis=1), jnp.concatenate(values, axis=0), (1, 0))
        near_copy(leaf).start()

    def own(leaf):
        return feat[leaf][:, LANES:], False, ordered[leaf]

    def inner(leaf):
        near(leaf, own(leaf - 1), own(leaf + 1))

    to_mate.wait_recv()
    each(forward, far[2:], lambda copy: copy.start())

    @pl.loop(1, 2)
    def _(leaf):
        inner(leaf)

    for copy in part_copies:
        copy.wait_recv()
    root = part_in[0].astype(F32)
    for j in range(1, subs):
        root = root + part_in[j].astype(F32)
    root = root.astype(BF16).astype(kind)
    top_low[...] = root
    top_all[top] = root
    top_copies = []
    for d in range(1, tops):
        copy = pltpu.make_async_remote_copy(
            src_ref=top_low, dst_ref=top_all.at[top],
            send_sem=top_send.at[d - 1], recv_sem=top_recv.at[d - 1],
            device_id={"leaf": lax.rem(top + d, tops)}, device_id_type=MESH,
        )
        copy.start()
        top_copies.append(copy)

    @pl.loop(2, 4)
    def _(leaf):
        inner(leaf)

    for n in range(2):
        @pl.when(within(sub - far[n]))
        def _():
            along(n).wait_recv()

    @pl.when(relays)
    def _():
        relay().start()

    for copy in top_copies:
        copy.wait_recv()
    field = jnp.zeros((width, rank), F32)
    for k in range(top_list.shape[1]):
        found = top_all[jnp.clip(top_list[0, k], 0, tops - 1)].astype(BF16)
        field = field + dot(found, top_ref[k], (1, 1))
    fields = [field]
    for level in reversed(range(levels)):
        first = 2 * subs - 2 * (subs >> level)
        fields = [
            dot(fields[j // 2].astype(BF16), level_ref[first + j], (1, 1)) for j in range(subs >> level)
        ]
    for j in range(subs):
        down_out[j] = fields[j].astype(kind)
    down_copies = deal(down_out, down_in, down_send, down_recv)

    @pl.loop(4, leaves - 1)
    def _(leaf):
        inner(leaf)

    for side in range(2):
        @pl.when(sends[1 - side])
        def _():
            for n in range(3):
                halo_copy(side, n).wait_recv()

    def halo(side):
        return sides(halo_feat[side].astype(F32))[1], True, halo_vals[side]

    near(0, halo(0), own(1))
    near(leaves - 1, own(leaves - 2), halo(1))

    for n in range(2, len(far)):
        @pl.when(within(sub - far[n]))
        def _():
            along(n).wait_recv()
            forward(n - 2).wait_recv()

    @pl.when(relayed)
    def _():
        relay().wait_recv()

    pair_field = jnp.zeros((rank, columns), F32)
    for k in range(pair_list.shape[1]):
        source = nodes[jnp.clip(pair_list[0, k] - top * subs, 0, subs - 1)]
        term = dot(pair_ref[k], source, (1, 0))
        pair_field = pair_field + jnp.where(k < pair_count[0], term, 0.0)

    for copy in down_copies:
        copy.wait_recv()
    turned = jnp.concatenate([down_in[j].astype(F32) for j in range(subs)], axis=0)
    field = (turned.T + pair_field).astype(BF16)
    field_ref[...] = field
    field_copy = pltpu.make_async_copy(field_ref, field_hbm, field_sem)
    field_copy.start()

    twice_copy.wait()
    field_copy.wait()
    for leaf in range(leaves):
        near_copy(leaf).wait()
    each(along, far, lambda copy: copy.wait_send())
    each(forward, far[2:], lambda copy: copy.wait_send())

    @pl.when(relays)
    def _():
        relay().wait_send()

    for copy in [to_mate] + part_copies + top_copies + down_copies:
        copy.wait_send()
    for side in range(2):
        @pl.when(sends[side])
        def _():
            for n in range(3):
                halo_copy(side, n).wait_send()


def scatter_kernel(
    twice_hbm, near_hbm, basis_hbm, transfer_hbm, field_hbm, out_hbm,
    twice_ref, near_ref, basis_ref, transfer_ref, field_ref, out_ref, leaf_field, even, odd,
    load_sem, near_sem, basis_sem, out_sem,
):
    leaves, rows, rank = basis_ref.shape
    lanes = out_ref.shape[1]
    loads = [
        pltpu.make_async_copy(src, dst, load_sem.at[n])
        for n, (src, dst) in enumerate((
            (field_hbm, field_ref), (transfer_hbm, transfer_ref), (twice_hbm, twice_ref),
        ))
    ]

    def leaf_loads(leaf):
        return (
            pltpu.make_async_copy(near_hbm.at[leaf], near_ref.at[leaf], near_sem.at[leaf]),
            pltpu.make_async_copy(basis_hbm.at[leaf], basis_ref.at[leaf], basis_sem.at[leaf]),
        )

    for load in loads:
        load.start()
    for load in leaf_loads(0):
        load.start()
    for load in loads[:2]:
        load.wait()
    for leaf in range(1, leaves):
        for load in leaf_loads(leaf):
            load.start()

    def widen(leaf):
        leaf_field[leaf] = dot(transfer_ref[leaf], field_ref[...], (1, 0)).astype(BF16)

    widen(0)
    loads[2].wait()
    step = SLICES * DEPTH
    chunks = rows // step

    def fill(target, leaf, chunk):
        place = pl.ds(chunk * step, step)
        total = near_ref[leaf, place] + dot(basis_ref[leaf, place], leaf_field[leaf], (1, 0))
        target[pl.ds(0, step, stride=2), :] = total[:, :lanes]
        target[pl.ds(1, step, stride=2), :] = total[:, lanes:]

    def spread(source, leaf, chunk):
        bases = [q * DEPTH for q in range(SLICES)]
        places = [twice_ref.at[pl.ds(leaf * rows + chunk * step + base, DEPTH)] for base in bases]
        for k in range(DEPTH):
            taken = [source[pl.ds(2 * (base + k), 2), :] for base in bases]
            for place, rows_of in zip(places, taken):
                out_ref[pl.ds(place[k], 2), :] = rows_of

    def emit(leaf, last):
        for chunk in range(chunks):
            if chunk + 1 < chunks:
                fill(mixed[(chunk + 1) % 2], leaf, chunk + 1)
            elif not last:
                fill(mixed[0], leaf + 1, 0)
            spread(mixed[chunk % 2], leaf, chunk)

    mixed = (even, odd)
    for load in leaf_loads(0):
        load.wait()
    fill(even, 0, 0)

    @pl.loop(0, leaves - 1)
    def _(leaf):
        for load in leaf_loads(leaf + 1):
            load.wait()
        widen(leaf + 1)
        emit(leaf, False)

    emit(leaves - 1, True)

    parts = out_sem.shape[0]
    size = out_ref.shape[0] // parts
    stores = [
        pltpu.make_async_copy(out_ref.at[pl.ds(n * size, size)], out_hbm.at[pl.ds(n * size, size)], out_sem.at[n])
        for n in range(parts)
    ]
    for store in stores:
        store.start()
    for store in stores:
        store.wait()


def per_device(
    subs, tops,
    points, vectors, inv_length, order, leaf_basis, leaf_transfer, level_transfer,
    near_list, near_count, pair_list, pair_count, pair_coupling, top_list, top_coupling,
):
    leaves, rows, rank = leaf_basis.shape
    count, features = points.shape
    lanes = vectors.shape[2]
    columns = vectors.shape[1] * lanes
    width = columns // subs
    kind = BF16 if width % 16 == 0 else F32
    order_flat = order.reshape(-1)

    operands = (
        order_flat, order_flat.reshape(-1, LANES), near_list.T, near_count, pair_list, pair_count, top_list,
        vectors, points.T, inv_length[None, :],
        leaf_basis, leaf_transfer, level_transfer[0], pair_coupling[0], top_coupling[0],
    )
    near_sum, field, twice = pl.pallas_call(
        functools.partial(near_kernel, subs, tops),
        name="near",
        out_shape=(
            jax.ShapeDtypeStruct((leaves, rows, columns), F32),
            jax.ShapeDtypeStruct((rank, columns), BF16),
            jax.ShapeDtypeStruct((count // LANES, LANES), jnp.int32),
        ),
        in_specs=[pl.BlockSpec(memory_space=pltpu.HBM)] * len(operands),
        out_specs=[pl.BlockSpec(memory_space=pltpu.HBM)] * 3,
        scratch_shapes=[
            *(pltpu.SMEM(v.shape, v.dtype) for v in (operands[0], *operands[2:7])),
            *(pltpu.VMEM(v.shape, v.dtype) for v in operands[7:]),
            pltpu.SemaphoreType.DMA((len(operands),)),
            pltpu.VMEM((leaves, rows, columns), F32),
            pltpu.SemaphoreType.DMA((leaves,)),
            pltpu.VMEM((rank, columns), BF16),
            pltpu.VMEM((count // LANES, LANES), jnp.int32),
            pltpu.SemaphoreType.DMA,
            pltpu.VMEM((count, 2, LANES), BF16),
            pltpu.VMEM((rows, 2, LANES), BF16),
            pltpu.VMEM((leaves, rows, columns), BF16),
            pltpu.VMEM((leaves, rows, 2 * LANES), BF16),
            pltpu.VMEM((2, features, rows), BF16),
            pltpu.VMEM((rank, columns), F32),
            pltpu.VMEM((rank, columns), BF16),
            pltpu.VMEM((2, features, rows), BF16),
            pltpu.VMEM((2, rows, columns), BF16),
            pltpu.VMEM((subs, rank, columns), BF16),
            pltpu.VMEM((subs, width, rank), kind),
            pltpu.VMEM((subs, width, rank), kind),
            pltpu.VMEM((width, rank), kind),
            pltpu.VMEM((tops, width, rank), kind),
            pltpu.VMEM((subs, width, rank), kind),
            pltpu.VMEM((subs, width, rank), kind),
            pltpu.SemaphoreType.DMA((subs - 1,)),
            pltpu.SemaphoreType.DMA((subs - 1,)),
            pltpu.SemaphoreType.DMA((subs - 1,)),
            pltpu.SemaphoreType.DMA((subs - 1,)),
            pltpu.SemaphoreType.DMA((REACH - 2,)),
            pltpu.SemaphoreType.DMA((REACH - 2,)),
            pltpu.SemaphoreType.DMA,
            pltpu.SemaphoreType.DMA((REACH,)),
            pltpu.SemaphoreType.DMA((REACH,)),
            pltpu.SemaphoreType.DMA((2,)),
            pltpu.SemaphoreType.DMA((2,)),
            pltpu.SemaphoreType.DMA((6,)),
            pltpu.SemaphoreType.DMA((6,)),
            pltpu.SemaphoreType.DMA((tops - 1,)),
            pltpu.SemaphoreType.DMA((tops - 1,)),
        ],
        compiler_params=pltpu.CompilerParams(
            collective_id=0, has_side_effects=True
        ),
    )(*operands)

    shares = (twice.reshape(-1), near_sum, leaf_basis, leaf_transfer, field)
    result = pl.pallas_call(
        scatter_kernel,
        name="scatter",
        out_shape=jax.ShapeDtypeStruct((count * 2, lanes), F32),
        in_specs=[pl.BlockSpec(memory_space=pltpu.HBM)] * len(shares),
        out_specs=pl.BlockSpec(memory_space=pltpu.HBM),
        scratch_shapes=[
            pltpu.SMEM((count,), jnp.int32),
            *(pltpu.VMEM(v.shape, v.dtype) for v in shares[1:]),
            pltpu.VMEM((count * 2, lanes), F32),
            pltpu.VMEM((leaves, rank, columns), BF16),
            pltpu.VMEM((SLICES * DEPTH * 2, lanes), F32),
            pltpu.VMEM((SLICES * DEPTH * 2, lanes), F32),
            pltpu.SemaphoreType.DMA((3,)),
            pltpu.SemaphoreType.DMA((leaves,)),
            pltpu.SemaphoreType.DMA((leaves,)),
            pltpu.SemaphoreType.DMA((leaves,)),
        ],
    )(*shares)
    return result.reshape(count, vectors.shape[1], lanes)


def solution(mesh):
    shape = dict(mesh.shape)
    both = ("leaf", "sub")
    return jax.shard_map(
        functools.partial(per_device, shape["sub"], shape["leaf"]),
        mesh=mesh,
        in_specs=(
            P(both, None), P(both, None, None), P(), P(both, None), P(both, None, None),
            P(both, None, None), P("leaf", None, None, None), P(both, None), P(both),
            P(both, None), P(both), P(both, None, None, None), P("leaf", None),
            P("leaf", None, None, None),
        ),
        out_specs=P(both, None, None),
        check_vma=False,
    )
```

```python
import functools
import math

import jax
import jax.numpy as jnp
from jax import lax
from jax.experimental import pallas as pl
from jax.experimental.pallas import tpu as pltpu
from jax.sharding import PartitionSpec as P

MESH = pl.DeviceIdType.MESH
LOG2E = math.log2(math.e)
F32 = jnp.float32
BF16 = jnp.bfloat16
LANES = 128
SLICES = 8
DEPTH = 16
STEP = 512
REACH = 4


def dot(a, b, dims):
    return lax.dot_general(a, b, ((dims[:1], dims[1:]), ((), ())), preferred_element_type=F32)


def bf16_parts(value):
    high = value.astype(BF16).astype(F32)
    rest = value - high
    mid = rest.astype(BF16).astype(F32)
    low = (rest - mid).astype(BF16).astype(F32)
    return high, mid, low


def tile_of(lhs, rhs, turned):
    return jnp.exp2(dot(lhs, rhs, (1, 0 if turned else 1))).astype(BF16)


def sides(x):
    features, count = x.shape
    half = bf16_parts((-0.5 * LOG2E) * jnp.sum(x * x, axis=0, keepdims=True))
    ones = jnp.ones((3, count), F32)
    pad = jnp.zeros((2, count), F32)
    rest = jnp.zeros((LANES - 3 * features - 8, count), F32)
    left = jnp.concatenate([*bf16_parts(x * LOG2E), jnp.concatenate([*half, ones, pad], axis=0), rest], axis=0)
    right = jnp.concatenate([x, x, x, jnp.concatenate([ones, *half, pad], axis=0), rest], axis=0)
    return left.astype(BF16), right.astype(BF16)


def take_rows(order_ref, table, start, out):
    step = SLICES * DEPTH

    @pl.loop(0, out.shape[0] // step)
    def _(i):
        bases = [i * step + q * DEPTH for q in range(SLICES)]
        places = [order_ref.at[pl.ds(start + base, DEPTH)] for base in bases]
        targets = [out.at[pl.ds(base, DEPTH)] for base in bases]
        for k in range(DEPTH):
            for place, target in zip(places, targets):
                target[k] = table[place[k]]


def split_rows(got, out, leaf):
    flat = got.reshape(2 * got.shape[0], LANES)
    for half in range(2):
        out[leaf, :, half * LANES:(half + 1) * LANES] = flat[pl.ds(half, got.shape[0], stride=2), :]


def near_kernel(
    subs, tops,
    order_hbm, twice_src, list_hbm, count_hbm, pairs_hbm, used_hbm, tops_hbm,
    vec_hbm, pts_hbm, inv_hbm, basis_hbm, transfer_hbm, level_hbm, pair_hbm, top_hbm,
    near_hbm, field_hbm, twice_hbm,
    order_ref, near_list, near_count, pair_list, pair_count, top_list,
    vec_ref, pts_ref, inv_ref, basis_ref, transfer_ref, level_ref, pair_ref, top_ref,
    load_sem, near_ref, near_sem,
    field_ref, order_vec, twice_sem, table, got, ordered, feat, edge_feat, node_sum, node_low,
    halo_feat, halo_vals, nodes, part_out, part_in, top_low, top_all, down_out, down_in,
    part_send, part_recv, down_send, down_recv, fore_send, fore_recv, field_sem,
    node_send, node_recv, pass_send, pass_recv, halo_send, halo_recv, top_send, top_recv,
):
    leaves, rows, rank = basis_ref.shape
    features, count = pts_ref.shape
    columns = ordered.shape[2]
    sub = lax.axis_index("sub")
    top = lax.axis_index("leaf")
    levels = subs.bit_length() - 1
    first_leaf = (top * subs + sub) * leaves
    mate = sub + 1 - 2 * lax.rem(sub, 2)

    loads = [
        pltpu.make_async_copy(src, dst, load_sem.at[n])
        for n, (src, dst) in enumerate((
            (vec_hbm, vec_ref), (order_hbm, order_ref), (basis_hbm, basis_ref),
            (transfer_hbm, transfer_ref), (pts_hbm, pts_ref), (inv_hbm, inv_ref),
            (twice_src, order_vec), (level_hbm, level_ref),
            (pair_hbm, pair_ref), (top_hbm, top_ref), (list_hbm, near_list),
            (count_hbm, near_count), (pairs_hbm, pair_list), (used_hbm, pair_count),
            (tops_hbm, top_list),
        ))
    ]
    for load in loads:
        load.start()

    nodes[...] = jnp.zeros(nodes.shape, BF16)
    barrier = pltpu.get_barrier_semaphore()
    for d in range(1, subs):
        pl.semaphore_signal(barrier, inc=1, device_id={"sub": lax.rem(sub + d, subs)}, device_id_type=MESH)
    for d in range(1, tops):
        pl.semaphore_signal(barrier, inc=1, device_id={"leaf": lax.rem(top + d, tops)}, device_id_type=MESH)

    def fetch(leaf):
        take_rows(order_ref, vec_ref, leaf * rows, got)
        split_rows(got, ordered, leaf)

    def lift(leaf):
        coef = dot(basis_ref[leaf], ordered[leaf], (0, 0)).astype(BF16)
        node_sum[...] = node_sum[...] + dot(transfer_ref[leaf], coef, (0, 0))

    node_sum[...] = jnp.zeros_like(node_sum)
    for load in loads[:2]:
        load.wait()
    fetch(leaves - 1)
    fetch(0)
    for load in loads[2:4]:
        load.wait()
    lift(leaves - 1)
    lift(0)

    @pl.loop(1, 2)
    def _(leaf):
        fetch(leaf)
        lift(leaf)

    pl.semaphore_wait(barrier, subs + tops - 2)

    def halo_copy(side, n):
        leaf, peer = (leaves - 1, sub + 1) if side == 0 else (0, sub - 1)
        early = rows * 5 // 16
        part = (pl.ds(0, early), pl.ds(early, rows - early))[n % 2]
        src, dst = (
            (ordered.at[leaf, part], halo_vals.at[side, part]),
            (ordered.at[leaf, part], halo_vals.at[side, part]),
            (edge_feat.at[side], halo_feat.at[side]),
        )[n]
        return pltpu.make_async_remote_copy(
            src_ref=src, dst_ref=dst,
            send_sem=halo_send.at[3 * side + n], recv_sem=halo_recv.at[3 * side + n],
            device_id={"sub": jnp.clip(peer, 0, subs - 1)}, device_id_type=MESH,
        )

    sends = (sub < subs - 1, sub > 0)
    for side in range(2):
        @pl.when(sends[side])
        def _():
            halo_copy(side, 0).start()

        @pl.when(jnp.logical_not(sends[1 - side]))
        def _():
            halo_feat[side] = jnp.zeros(halo_feat.shape[1:], BF16)
            halo_vals[side] = jnp.zeros(halo_vals.shape[1:], BF16)

    @pl.loop(2, leaves - 1)
    def _(leaf):
        fetch(leaf)
        lift(leaf)

    node = node_sum[...].astype(BF16)
    node_low[...] = node
    nodes[sub] = node

    for load in loads[4:]:
        load.wait()

    width = columns // subs
    kind = part_out.dtype
    raised = dot(node, level_ref[sub], (0, 0))
    for level in range(1, levels):
        place = 2 * subs - 2 * (subs >> level) + jnp.right_shift(sub, level)
        raised = dot(raised.astype(BF16), level_ref[place], (1, 0))
    for j in range(subs):
        part_out[j] = raised[j * width:(j + 1) * width].astype(kind)

    def deal(source, target, sends_to, recvs):
        copies = []
        for d in range(1, subs):
            peer = lax.rem(sub + d, subs)
            copies.append(pltpu.make_async_remote_copy(
                src_ref=source.at[peer], dst_ref=target.at[sub],
                send_sem=sends_to.at[d - 1], recv_sem=recvs.at[d - 1],
                device_id={"sub": peer}, device_id_type=MESH,
            ))
        for copy in copies:
            copy.start()
        target[sub] = source[sub]
        return copies

    part_copies = deal(part_out, part_in, part_send, part_recv)

    def node_copy(n, src, dst, peer, sends_to, recvs):
        return pltpu.make_async_remote_copy(
            src_ref=src, dst_ref=dst, send_sem=sends_to.at[n], recv_sem=recvs.at[n],
            device_id={"sub": peer}, device_id_type=MESH,
        )

    def within(place):
        return (place >= 0) & (place < subs)

    def inside(place):
        return jnp.clip(place, 0, subs - 1)

    far = tuple(d for step in range(REACH, 0, -2) for d in (step, -step))
    parity = lax.rem(sub, 2)

    def along(n):
        return node_copy(n, node_low, nodes.at[sub], inside(sub + far[n]), node_send, node_recv)

    def forward(n):
        return node_copy(n, nodes.at[mate], nodes.at[mate], inside(sub + far[2 + n]), fore_send, fore_recv)

    def relay():
        origin = inside(sub + REACH - 2 * REACH * parity)
        return node_copy(1, nodes.at[origin], nodes.at[origin], mate, pass_send, pass_recv)

    relays = within(sub + REACH - 2 * REACH * parity)
    relayed = within(mate - REACH + 2 * REACH * parity)

    def each(make, spans, act):
        for n, span in enumerate(spans):
            @pl.when(within(sub + span))
            def _():
                act(make(n))

    to_mate = node_copy(0, node_low, nodes.at[sub], mate, pass_send, pass_recv)
    to_mate.start()
    each(along, far, lambda copy: copy.start())
    for side in range(2):
        @pl.when(sends[side])
        def _():
            halo_copy(side, 1).start()

    order_vec[...] = order_vec[...] * 2
    twice_copy = pltpu.make_async_copy(order_vec, twice_hbm, twice_sem)
    twice_copy.start()

    square = (features, features)
    same = lax.broadcasted_iota(jnp.int32, square, 0) == lax.broadcasted_iota(jnp.int32, square, 1)
    inv = jnp.sum(jnp.where(same, jnp.broadcast_to(inv_ref[...], square), 0.0), axis=1, keepdims=True)

    @pl.loop(0, count // STEP)
    def _(i):
        for part in range(STEP // LANES):
            start = pl.multiple_of(i * STEP + part * LANES, LANES)
            x = (pts_ref[:, pl.ds(start, LANES)].astype(F32) * inv).astype(BF16).astype(F32)
            both = jnp.concatenate(sides(x), axis=0).T
            table[pl.ds(start, LANES)] = both.reshape(LANES, 2, LANES)

    def features_of(leaf):
        take_rows(order_ref, table, leaf * rows, got)
        split_rows(got, feat, leaf)

    for side, leaf in ((0, leaves - 1), (1, 0)):
        features_of(leaf)
        edge_feat[side] = feat[leaf][:, LANES:].T[:features]

        @pl.when(sends[side])
        def _():
            halo_copy(side, 2).start()

    @pl.loop(1, leaves // 2)
    def _(leaf):
        features_of(leaf)

    @pl.loop(leaves // 2, leaves - 1)
    def _(leaf):
        features_of(leaf)

    def wanted(leaf, target):
        found = jnp.int32(0)
        for k in range(near_list.shape[0]):
            found = found | ((near_list[k, leaf] == target) & (k < near_count[leaf])).astype(jnp.int32)
        return found.astype(F32).astype(BF16)

    def near_copy(leaf):
        return pltpu.make_async_copy(near_ref.at[leaf], near_hbm.at[leaf], near_sem.at[leaf])

    def near(leaf, before, after):
        flag_before = wanted(leaf, first_leaf + leaf - 1)
        flag_after = wanted(leaf, first_leaf + leaf + 1)
        tiles, values = [], []
        for (rhs, turned, vals), flag in (
            ((feat[leaf][:, LANES:], False, ordered[leaf]), None),
            (before, flag_before),
            (after, flag_after),
        ):
            tiles.append(tile_of(feat[leaf][:, :LANES], rhs, turned))
            values.append(vals if flag is None else vals * flag)
        near_ref[leaf] = dot(jnp.concatenate(tiles, axis=1), jnp.concatenate(values, axis=0), (1, 0))
        near_copy(leaf).start()

    def own(leaf):
        return feat[leaf][:, LANES:], False, ordered[leaf]

    def inner(leaf):
        near(leaf, own(leaf - 1), own(leaf + 1))

    to_mate.wait_recv()
    each(forward, far[2:], lambda copy: copy.start())

    @pl.loop(1, 2)
    def _(leaf):
        inner(leaf)

    for copy in part_copies:
        copy.wait_recv()
    root = part_in[0].astype(F32)
    for j in range(1, subs):
        root = root + part_in[j].astype(F32)
    root = root.astype(BF16).astype(kind)
    top_low[...] = root
    top_all[top] = root
    top_copies = []
    for d in range(1, tops):
        copy = pltpu.make_async_remote_copy(
            src_ref=top_low, dst_ref=top_all.at[top],
            send_sem=top_send.at[d - 1], recv_sem=top_recv.at[d - 1],
            device_id={"leaf": lax.rem(top + d, tops)}, device_id_type=MESH,
        )
        copy.start()
        top_copies.append(copy)

    @pl.loop(2, 4)
    def _(leaf):
        inner(leaf)

    for n in range(2):
        @pl.when(within(sub - far[n]))
        def _():
            along(n).wait_recv()

    @pl.when(relays)
    def _():
        relay().start()

    for copy in top_copies:
        copy.wait_recv()
    field = jnp.zeros((width, rank), F32)
    for k in range(top_list.shape[1]):
        found = top_all[jnp.clip(top_list[0, k], 0, tops - 1)].astype(BF16)
        field = field + dot(found, top_ref[k], (1, 1))
    fields = [field]
    for level in reversed(range(levels)):
        first = 2 * subs - 2 * (subs >> level)
        fields = [
            dot(fields[j // 2].astype(BF16), level_ref[first + j], (1, 1)) for j in range(subs >> level)
        ]
    for j in range(subs):
        down_out[j] = fields[j].astype(kind)
    down_copies = deal(down_out, down_in, down_send, down_recv)

    @pl.loop(4, leaves - 1)
    def _(leaf):
        inner(leaf)

    for side in range(2):
        @pl.when(sends[1 - side])
        def _():
            for n in range(3):
                halo_copy(side, n).wait_recv()

    def halo(side):
        return sides(halo_feat[side].astype(F32))[1], True, halo_vals[side]

    near(0, halo(0), own(1))
    near(leaves - 1, own(leaves - 2), halo(1))

    for n in range(2, len(far)):
        @pl.when(within(sub - far[n]))
        def _():
            along(n).wait_recv()
            forward(n - 2).wait_recv()

    @pl.when(relayed)
    def _():
        relay().wait_recv()

    pair_field = jnp.zeros((rank, columns), F32)
    for k in range(pair_list.shape[1]):
        source = nodes[jnp.clip(pair_list[0, k] - top * subs, 0, subs - 1)]
        term = dot(pair_ref[k], source, (1, 0))
        pair_field = pair_field + jnp.where(k < pair_count[0], term, 0.0)

    for copy in down_copies:
        copy.wait_recv()
    turned = jnp.concatenate([down_in[j].astype(F32) for j in range(subs)], axis=0)
    field = (turned.T + pair_field).astype(BF16)
    field_ref[...] = field
    field_copy = pltpu.make_async_copy(field_ref, field_hbm, field_sem)
    field_copy.start()

    twice_copy.wait()
    field_copy.wait()
    for leaf in range(leaves):
        near_copy(leaf).wait()
    each(along, far, lambda copy: copy.wait_send())
    each(forward, far[2:], lambda copy: copy.wait_send())

    @pl.when(relays)
    def _():
        relay().wait_send()

    for copy in [to_mate] + part_copies + top_copies + down_copies:
        copy.wait_send()
    for side in range(2):
        @pl.when(sends[side])
        def _():
            for n in range(3):
                halo_copy(side, n).wait_send()


def scatter_kernel(
    twice_hbm, near_hbm, basis_hbm, transfer_hbm, field_hbm, out_hbm,
    twice_ref, near_ref, basis_ref, transfer_ref, field_ref, out_ref, leaf_field, even, odd,
    load_sem, near_sem, basis_sem, out_sem,
):
    leaves, rows, rank = basis_ref.shape
    lanes = out_ref.shape[1]
    loads = [
        pltpu.make_async_copy(src, dst, load_sem.at[n])
        for n, (src, dst) in enumerate((
            (field_hbm, field_ref), (transfer_hbm, transfer_ref), (twice_hbm, twice_ref),
        ))
    ]

    def leaf_loads(leaf):
        return (
            pltpu.make_async_copy(near_hbm.at[leaf], near_ref.at[leaf], near_sem.at[leaf]),
            pltpu.make_async_copy(basis_hbm.at[leaf], basis_ref.at[leaf], basis_sem.at[leaf]),
        )

    for load in loads:
        load.start()
    for load in leaf_loads(0):
        load.start()
    for load in loads[:2]:
        load.wait()
    for leaf in range(1, leaves):
        for load in leaf_loads(leaf):
            load.start()

    def widen(leaf):
        leaf_field[leaf] = dot(transfer_ref[leaf], field_ref[...], (1, 0)).astype(BF16)

    widen(0)
    loads[2].wait()
    step = SLICES * DEPTH
    chunks = rows // step

    def fill(target, leaf, chunk):
        place = pl.ds(chunk * step, step)
        total = near_ref[leaf, place] + dot(basis_ref[leaf, place], leaf_field[leaf], (1, 0))
        target[pl.ds(0, step, stride=2), :] = total[:, :lanes]
        target[pl.ds(1, step, stride=2), :] = total[:, lanes:]

    def spread(source, leaf, chunk):
        bases = [q * DEPTH for q in range(SLICES)]
        places = [twice_ref.at[pl.ds(leaf * rows + chunk * step + base, DEPTH)] for base in bases]
        for k in range(DEPTH):
            taken = [source[pl.ds(2 * (base + k), 2), :] for base in bases]
            for place, rows_of in zip(places, taken):
                out_ref[pl.ds(place[k], 2), :] = rows_of

    def emit(leaf, last):
        for chunk in range(chunks):
            if chunk + 1 < chunks:
                fill(mixed[(chunk + 1) % 2], leaf, chunk + 1)
            elif not last:
                fill(mixed[0], leaf + 1, 0)
            spread(mixed[chunk % 2], leaf, chunk)

    mixed = (even, odd)
    for load in leaf_loads(0):
        load.wait()
    fill(even, 0, 0)

    @pl.loop(0, leaves - 1)
    def _(leaf):
        for load in leaf_loads(leaf + 1):
            load.wait()
        widen(leaf + 1)
        emit(leaf, False)

    emit(leaves - 1, True)

    parts = out_sem.shape[0]
    size = out_ref.shape[0] // parts
    stores = [
        pltpu.make_async_copy(out_ref.at[pl.ds(n * size, size)], out_hbm.at[pl.ds(n * size, size)], out_sem.at[n])
        for n in range(parts)
    ]
    for store in stores:
        store.start()
    for store in stores:
        store.wait()


def per_device(
    subs, tops,
    points, vectors, inv_length, order, leaf_basis, leaf_transfer, level_transfer,
    near_list, near_count, pair_list, pair_count, pair_coupling, top_list, top_coupling,
):
    leaves, rows, rank = leaf_basis.shape
    count, features = points.shape
    lanes = vectors.shape[2]
    columns = vectors.shape[1] * lanes
    width = columns // subs
    kind = BF16 if width % 16 == 0 else F32
    order_flat = order.reshape(-1)

    operands = (
        order_flat, order_flat.reshape(-1, LANES), near_list.T, near_count, pair_list, pair_count, top_list,
        vectors, points.T, inv_length[None, :],
        leaf_basis, leaf_transfer, level_transfer[0], pair_coupling[0], top_coupling[0],
    )
    near_sum, field, twice = pl.pallas_call(
        functools.partial(near_kernel, subs, tops),
        name="near",
        out_shape=(
            jax.ShapeDtypeStruct((leaves, rows, columns), F32),
            jax.ShapeDtypeStruct((rank, columns), BF16),
            jax.ShapeDtypeStruct((count // LANES, LANES), jnp.int32),
        ),
        in_specs=[pl.BlockSpec(memory_space=pltpu.HBM)] * len(operands),
        out_specs=[pl.BlockSpec(memory_space=pltpu.HBM)] * 3,
        scratch_shapes=[
            *(pltpu.SMEM(v.shape, v.dtype) for v in (operands[0], *operands[2:7])),
            *(pltpu.VMEM(v.shape, v.dtype) for v in operands[7:]),
            pltpu.SemaphoreType.DMA((len(operands),)),
            pltpu.VMEM((leaves, rows, columns), F32),
            pltpu.SemaphoreType.DMA((leaves,)),
            pltpu.VMEM((rank, columns), BF16),
            pltpu.VMEM((count // LANES, LANES), jnp.int32),
            pltpu.SemaphoreType.DMA,
            pltpu.VMEM((count, 2, LANES), BF16),
            pltpu.VMEM((rows, 2, LANES), BF16),
            pltpu.VMEM((leaves, rows, columns), BF16),
            pltpu.VMEM((leaves, rows, 2 * LANES), BF16),
            pltpu.VMEM((2, features, rows), BF16),
            pltpu.VMEM((rank, columns), F32),
            pltpu.VMEM((rank, columns), BF16),
            pltpu.VMEM((2, features, rows), BF16),
            pltpu.VMEM((2, rows, columns), BF16),
            pltpu.VMEM((subs, rank, columns), BF16),
            pltpu.VMEM((subs, width, rank), kind),
            pltpu.VMEM((subs, width, rank), kind),
            pltpu.VMEM((width, rank), kind),
            pltpu.VMEM((tops, width, rank), kind),
            pltpu.VMEM((subs, width, rank), kind),
            pltpu.VMEM((subs, width, rank), kind),
            pltpu.SemaphoreType.DMA((subs - 1,)),
            pltpu.SemaphoreType.DMA((subs - 1,)),
            pltpu.SemaphoreType.DMA((subs - 1,)),
            pltpu.SemaphoreType.DMA((subs - 1,)),
            pltpu.SemaphoreType.DMA((REACH - 2,)),
            pltpu.SemaphoreType.DMA((REACH - 2,)),
            pltpu.SemaphoreType.DMA,
            pltpu.SemaphoreType.DMA((REACH,)),
            pltpu.SemaphoreType.DMA((REACH,)),
            pltpu.SemaphoreType.DMA((2,)),
            pltpu.SemaphoreType.DMA((2,)),
            pltpu.SemaphoreType.DMA((6,)),
            pltpu.SemaphoreType.DMA((6,)),
            pltpu.SemaphoreType.DMA((tops - 1,)),
            pltpu.SemaphoreType.DMA((tops - 1,)),
        ],
        compiler_params=pltpu.CompilerParams(
            collective_id=0, has_side_effects=True
        ),
    )(*operands)

    shares = (twice.reshape(-1), near_sum, leaf_basis, leaf_transfer, field)
    result = pl.pallas_call(
        scatter_kernel,
        name="scatter",
        out_shape=jax.ShapeDtypeStruct((count * 2, lanes), F32),
        in_specs=[pl.BlockSpec(memory_space=pltpu.HBM)] * len(shares),
        out_specs=pl.BlockSpec(memory_space=pltpu.HBM),
        scratch_shapes=[
            pltpu.SMEM((count,), jnp.int32),
            *(pltpu.VMEM(v.shape, v.dtype) for v in shares[1:]),
            pltpu.VMEM((count * 2, lanes), F32),
            pltpu.VMEM((leaves, rank, columns), BF16),
            pltpu.VMEM((SLICES * DEPTH * 2, lanes), F32),
            pltpu.VMEM((SLICES * DEPTH * 2, lanes), F32),
            pltpu.SemaphoreType.DMA((3,)),
            pltpu.SemaphoreType.DMA((leaves,)),
            pltpu.SemaphoreType.DMA((leaves,)),
            pltpu.SemaphoreType.DMA((leaves,)),
        ],
    )(*shares)
    return result.reshape(count, vectors.shape[1], lanes)


def solution(mesh):
    shape = dict(mesh.shape)
    both = ("leaf", "sub")
    return jax.shard_map(
        functools.partial(per_device, shape["sub"], shape["leaf"]),
        mesh=mesh,
        in_specs=(
            P(both, None), P(both, None, None), P(), P(both, None), P(both, None, None),
            P(both, None, None), P("leaf", None, None, None), P(both, None), P(both),
            P(both, None), P(both), P(both, None, None, None), P("leaf", None),
            P("leaf", None, None, None),
        ),
        out_specs=P(both, None, None),
        check_vma=False,
    )
```
